32 devices in a mesh: groups: 2 (over y), tiles: 4 (over z), rhs: 2 (over x), sub: 2 (over core).
Axes of the slice: x: 2, y: 2, z: 4, core: 2. Of those that a mesh axis runs over, the one named last changes fastest.
Arguments:
- sources: bfloat16 [256, 8192], P('rhs', ('groups', 'tiles', 'sub')), parts along dimension 1, may hold values from -6 to 6
- basis_out: bfloat16 [384, 64, 512], P(('groups', 'tiles', 'rhs', 'sub')), parts along dimension 0, may hold values from -0.15625 to 0.15625
- basis_in: bfloat16 [384, 64, 512], P(('groups', 'tiles', 'rhs', 'sub')), parts along dimension 0, may hold values from -0.25 to 0.25
- tile_rank: int32 [384], P(('groups', 'tiles', 'rhs', 'sub')), parts along dimension 0, may hold values from 1 to 64, as said below
- tile_row: int32 [384], P(('groups', 'tiles', 'rhs', 'sub')), parts along dimension 0, may hold values from 0 to 7
- tile_col: int32 [384], P(('groups', 'tiles', 'rhs', 'sub')), parts along dimension 0, may hold values from 0 to 7
- near_blocks: bfloat16 [16, 16, 512, 512], P(('groups', 'tiles', 'sub')), parts along dimension 0, may hold values from -0.0625 to 0.0625
- near_col: int32 [16, 16], P(('groups', 'tiles', 'sub')), parts along dimension 0, may hold values from 0 to 7
- jacobi_inverse: bfloat16 [64, 128, 128], P(('groups', 'tiles', 'sub')), parts along dimension 0
Outputs:
- first_result: bfloat16 [256, 8192], P('rhs', ('groups', 'tiles', 'sub')), parts along dimension 1
- second_result: bfloat16 [256, 8192], P('rhs', ('groups', 'tiles', 'sub')), parts along dimension 1
The draws below stay inside these ranges and needn't reach their ends.
There are 2 independent parts, one for each index of `groups`. The reference program is written for one: setup_inputs(seed, part) draws one part's arguments, and reference() takes and returns one part's arrays. A program takes and returns all parts, laid end to end along the dimension named above; each array names one. Nothing has to cross between parts.
Inputs may be any that keep to these rules, and one draw needn't show every extreme that they name: `tile_rank`: every rank lies in 1 to 64, and some tile has rank 64.
All inputs are finite; a program needn't handle non-finite values.
Results may differ from the reference program's by a relative error of at most 0.03.
Values may be sent and summed in bfloat16 or wider, within the bound.
No kernel may reach another device: no remote copies, remote signals or barrier semaphores. Data moves between devices by JAX's collectives and lax.ppermute only.
A program may use at most 128 MiB of HBM per device.

```python
import jax
import jax.numpy as jnp
from jax import lax

BLK = 512
RMAX = 64
JB = 128
NRHS = 256
NEAR = 16
NB_DEV = 1
TILE_DEV = 12
NB = 8
NPAN = 4096
NT = 192
NG = 32
N_RHS = 2


def draw_tile_rank(key, part):
    first_key = jax.random.fold_in(key, 11)
    second_key = jax.random.fold_in(key, 12)
    ranks = jax.random.randint(first_key, (NT,), 1, RMAX + 1, dtype=jnp.int32)
    position = jax.random.randint(second_key, (), 0, NT, dtype=jnp.int32)
    return jnp.where(jnp.arange(NT, dtype=jnp.int32) == position, RMAX, ranks).astype(jnp.int32)


def draw_jacobi_inverse(key, part):
    noise_key = jax.random.fold_in(key, 21)
    noise = jax.random.normal(noise_key, (NG, JB, JB), jnp.float32) * 0.5
    identity = jnp.eye(JB, dtype=jnp.float32)[None, :, :]
    return (identity + noise / JB ** 0.5).astype(jnp.bfloat16)


def plant(drawn, rng, smallest, top_value):
    place = [jax.random.randint(jax.random.fold_in(rng, axis), (), 0, length) for axis, length in enumerate(drawn.shape)]
    widest = drawn.shape.index(max(drawn.shape))
    next_to = place[:widest] + [(place[widest] + 1) % drawn.shape[widest]] + place[widest + 1:]
    return drawn.at[tuple(place)].set(smallest).at[tuple(next_to)].set(top_value)


def shard_levels(own_key, dims, shards, smallest, top_value):
    loudness = 1.0
    for dim, blocks in shards:
        draws = jax.random.uniform(jax.random.fold_in(jax.random.fold_in(own_key, 6), dim), (blocks,), jnp.float32, smallest / len(shards), top_value / len(shards))
        loudness = loudness * jnp.repeat(jnp.exp(draws), dims[dim] // blocks).reshape((-1,) + (1,) * (len(dims) - 1 - dim))
    return loudness


def centred(stream_key, dims, width, most, cuts=(), kind=jnp.bfloat16):
    drawn = width * jax.random.normal(stream_key, dims, jnp.float32)
    if cuts:
        drawn = drawn * shard_levels(stream_key, dims, cuts, -0.22, 0.18)
    return jnp.clip(drawn, -most, most).astype(kind)


def setup_inputs(seed: int = 0, part: int = 0) -> dict:
    keys = jax.random.split(jax.random.key(seed), 10)
    own_keys = jax.random.split(jax.random.fold_in(keys[9], part), 10)
    sources = centred(own_keys[0], (NRHS, NPAN), 1.0, 6.0, ((0, 2), (1, 8)))
    basis_out = centred(own_keys[1], (NT, RMAX, BLK), (RMAX * TILE_DEV * N_RHS // NB_DEV) ** -0.5, 0.15625, ((0, 16),))
    basis_in = centred(own_keys[2], (NT, RMAX, BLK), BLK ** -0.5, 0.25, ((0, 16),))
    tile_rank = draw_tile_rank(jax.random.fold_in(jax.random.fold_in(keys[9], part), 71), part)
    tile_row = plant(jax.random.randint(own_keys[4], (NT,), 0, NB), jax.random.fold_in(own_keys[4], 1), 0, NB - 1).astype(jnp.int32)
    tile_col = plant(jax.random.randint(own_keys[5], (NT,), 0, NB), jax.random.fold_in(own_keys[5], 1), 0, NB - 1).astype(jnp.int32)
    near_blocks = centred(own_keys[6], (NB, NEAR, BLK, BLK), (NEAR * BLK) ** -0.5, 0.0625, ((0, 8),))
    near_col = plant(jax.random.randint(own_keys[7], (NB, NEAR), 0, NB), jax.random.fold_in(own_keys[7], 1), 0, NB - 1).astype(jnp.int32)
    jacobi_inverse = draw_jacobi_inverse(jax.random.fold_in(jax.random.fold_in(keys[9], part), 71), part)
    return dict(sources=sources, basis_out=basis_out, basis_in=basis_in, tile_rank=tile_rank, tile_row=tile_row, tile_col=tile_col, near_blocks=near_blocks, near_col=near_col, jacobi_inverse=jacobi_inverse)


def apply_operator(vector, basis_out, basis_in, tile_rank, tile_row, tile_col, near_blocks, near_col):
    blocks = vector.reshape(NRHS, NB, BLK).transpose(1, 0, 2)

    def add_tile(running, index):
        coefficients = jnp.dot(blocks[tile_col[index]], basis_in[index].T, preferred_element_type=jnp.float32)
        kept_mask = jnp.arange(RMAX, dtype=jnp.int32) < tile_rank[index]
        coefficients = jnp.where(kept_mask[None, :], coefficients, jnp.zeros_like(coefficients)).astype(jnp.bfloat16)
        contrib = jnp.dot(coefficients, basis_out[index], preferred_element_type=jnp.float32)
        return running.at[tile_row[index]].add(contrib), None

    far_field, unused = lax.scan(add_tile, jnp.zeros((NB, NRHS, BLK), jnp.float32), jnp.arange(NT, dtype=jnp.int32))

    def near_row(index):
        picked = blocks[near_col[index]].astype(jnp.float32)
        return jnp.einsum('kcq,kpq->cp', picked, near_blocks[index].astype(jnp.float32))

    near_field = lax.map(near_row, jnp.arange(NB, dtype=jnp.int32))
    summed = (far_field + near_field).astype(jnp.bfloat16)
    return summed.transpose(1, 0, 2).reshape(NRHS, NPAN)


def precondition(field, jacobi_inverse):
    grouped = field.reshape(NRHS, NG, JB).astype(jnp.float32)
    result = jnp.einsum('cgq,gpq->cgp', grouped, jacobi_inverse.astype(jnp.float32))
    return result.astype(jnp.bfloat16).reshape(NRHS, NPAN)


def reference(sources, basis_out, basis_in, tile_rank, tile_row, tile_col, near_blocks, near_col, jacobi_inverse):
    first_result = precondition(apply_operator(sources, basis_out, basis_in, tile_rank, tile_row, tile_col, near_blocks, near_col), jacobi_inverse)
    second_result = precondition(apply_operator(first_result, basis_out, basis_in, tile_rank, tile_row, tile_col, near_blocks, near_col), jacobi_inverse)
    return (first_result, second_result)
```

```python
import functools

import jax
import jax.numpy as jnp
from jax import lax
from jax.experimental import pallas as pl
from jax.experimental.pallas import tpu as pltpu
from jax.sharding import PartitionSpec as P

BLK = 512
RMAX = 64
JB = 128
NCHUNK = 256
BF16 = jnp.bfloat16
F32 = jnp.float32
VMEM_LIMIT = 48 * 1024 * 1024
CONTRACT_LAST = (((1,), (1,)), ((), ()))


def shifted(value, axis, size, amount):
    return lax.ppermute(value, axis, [(i, (i + amount) % size) for i in range(size)])


def fetch(pieces, stacked, sems):
    rows = pieces[0].shape[0]
    copies = [
        pltpu.make_async_copy(piece, stacked.at[pl.ds(i * rows, rows)], sems.at[i])
        for i, piece in enumerate(pieces)
    ]
    for copy in copies:
        copy.start()
    for copy in copies:
        copy.wait()


def far_kernel(n_pieces, n_parts, n_keep, col_ref, row_ref, *refs):
    pieces = refs[:n_pieces]
    ins = refs[n_pieces : n_pieces + n_parts]
    outs = refs[n_pieces + n_parts : n_pieces + 2 * n_parts]
    keep_ref, send_ref, stacked, coeff, masked, sems = refs[n_pieces + 2 * n_parts :]
    rows = pieces[0].shape[0]
    width = ins[0].shape[0]
    fetch(pieces, stacked, sems)
    for part in range(n_parts):
        for chunk in range(width // NCHUNK):
            here = pl.ds(chunk * NCHUNK, NCHUNK)
            there = pl.ds(part * width + chunk * NCHUNK, NCHUNK)
            products = lax.dot_general(
                stacked[...], ins[part][here, :], CONTRACT_LAST, preferred_element_type=F32
            )
            column = col_ref[:, there]
            chosen = products[:rows]
            for piece in range(1, n_pieces):
                chosen = jnp.where(
                    column == piece, products[piece * rows : (piece + 1) * rows], chosen
                )
            coeff[:, there] = chosen
    for target in range(n_pieces):
        for chunk in range(n_parts * width // NCHUNK):
            there = pl.ds(chunk * NCHUNK, NCHUNK)
            masked[pl.ds(target * rows, rows), there] = jnp.where(
                row_ref[:, there] == target, coeff[:, there], 0.0
            ).astype(BF16)
    total = jnp.dot(masked[:, :width], outs[0][...], preferred_element_type=F32)
    for part in range(1, n_parts):
        total += jnp.dot(
            masked[:, part * width : (part + 1) * width],
            outs[part][...],
            preferred_element_type=F32,
        )
    total = total.astype(BF16)
    keep_ref[...] = total[: n_keep * rows]
    send_ref[...] = total[n_keep * rows :]


def far_field(pieces, ins, outs, columns, rows_of, n_keep):
    rows = pieces[0].shape[0]
    n_pieces, n_parts, width = len(pieces), len(ins), ins[0].shape[0]
    whole = pl.BlockSpec(memory_space=pltpu.VMEM)
    anywhere = pl.BlockSpec(memory_space=pl.ANY)
    flops = 4 * n_pieces * rows * n_parts * width * BLK
    return pl.pallas_call(
        functools.partial(far_kernel, n_pieces, n_parts, n_keep),
        out_shape=(
            jax.ShapeDtypeStruct((n_keep * rows, BLK), BF16),
            jax.ShapeDtypeStruct(((n_pieces - n_keep) * rows, BLK), BF16),
        ),
        in_specs=[whole, whole] + [anywhere] * n_pieces + [whole] * (2 * n_parts),
        out_specs=(whole, whole),
        scratch_shapes=[
            pltpu.VMEM((n_pieces * rows, BLK), BF16),
            pltpu.VMEM((rows, n_parts * width), F32),
            pltpu.VMEM((n_pieces * rows, n_parts * width), BF16),
            pltpu.SemaphoreType.DMA((n_pieces,)),
        ],
        compiler_params=pltpu.CompilerParams(vmem_limit_bytes=VMEM_LIMIT),
        cost_estimate=pl.CostEstimate(
            flops=flops,
            transcendentals=0,
            bytes_accessed=2 * BLK * (2 * n_pieces * rows + 2 * n_parts * width),
        ),
        name="far_field",
    )(columns, rows_of, *pieces, *ins, *outs)


def near_kernel(n_pieces, per_step, slot_ref, *refs):
    pieces = refs[:n_pieces]
    blocks_ref, out_ref, stacked, sems = refs[n_pieces:]
    rows = pieces[0].shape[0]
    step = pl.program_id(0)

    @pl.when(step == 0)
    def _():
        fetch(pieces, stacked, sems)
        out_ref[...] = jnp.zeros_like(out_ref)

    total = out_ref[...]
    for k in range(per_step):
        start = pl.multiple_of(slot_ref[step * per_step + k] * rows, rows)
        total += lax.dot_general(
            stacked[pl.ds(start, rows), :],
            blocks_ref[k],
            CONTRACT_LAST,
            preferred_element_type=F32,
        )
    out_ref[...] = total


def near_field(pieces, near_blocks, slots):
    rows = pieces[0].shape[0]
    n_pieces, near = len(pieces), near_blocks.shape[0]
    per_step = 4 if near % 4 == 0 else 1
    anywhere = pl.BlockSpec(memory_space=pl.ANY)
    return pl.pallas_call(
        functools.partial(near_kernel, n_pieces, per_step),
        out_shape=jax.ShapeDtypeStruct((rows, BLK), F32),
        grid_spec=pltpu.PrefetchScalarGridSpec(
            num_scalar_prefetch=1,
            grid=(near // per_step,),
            in_specs=[anywhere] * n_pieces
            + [pl.BlockSpec((per_step, BLK, BLK), lambda step, slot: (step, 0, 0))],
            out_specs=pl.BlockSpec((rows, BLK), lambda step, slot: (0, 0)),
            scratch_shapes=[
                pltpu.VMEM((n_pieces * rows, BLK), BF16),
                pltpu.SemaphoreType.DMA((n_pieces,)),
            ],
        ),
        compiler_params=pltpu.CompilerParams(vmem_limit_bytes=VMEM_LIMIT),
        cost_estimate=pl.CostEstimate(
            flops=2 * near * rows * BLK * BLK,
            transcendentals=0,
            bytes_accessed=2 * BLK * (near * BLK + n_pieces * rows + 2 * rows),
        ),
        name="near_field",
    )(slots, *pieces, near_blocks)


def finish_kernel(n_sums, *refs):
    sums, (near_ref, jacobi_ref, out_ref) = refs[:n_sums], refs[n_sums:]
    total = near_ref[...]
    for part in sums:
        total += part[...].astype(F32)
    field = total.astype(BF16)
    for group in range(jacobi_ref.shape[0]):
        here = slice(group * JB, (group + 1) * JB)
        out_ref[:, here] = lax.dot_general(
            field[:, here], jacobi_ref[group], CONTRACT_LAST, preferred_element_type=F32
        ).astype(BF16)


def finish(sums, near, jacobi_inverse):
    whole = pl.BlockSpec(memory_space=pltpu.VMEM)
    return pl.pallas_call(
        functools.partial(finish_kernel, len(sums)),
        out_shape=jax.ShapeDtypeStruct(near.shape, BF16),
        in_specs=[whole] * (len(sums) + 2),
        out_specs=whole,
        name="finish",
    )(*sums, near, jacobi_inverse)


def local(
    n_tiles,
    n_rhs,
    n_sub,
    sources,
    basis_out,
    basis_in,
    tile_rank,
    tile_row,
    tile_col,
    near_blocks,
    near_col,
    jacobi_inverse,
):
    z = lax.axis_index("tiles")
    s = lax.axis_index("sub")
    rows = sources.shape[0]
    basis_in = basis_in.reshape(-1, BLK)
    basis_out = basis_out.reshape(-1, BLK)

    def source_slot(block):
        return (s - block % n_sub) % n_sub * n_tiles + (z - block // n_sub) % n_tiles

    def target_slot(block):
        return (block % n_sub - s) % n_sub * n_tiles + (block // n_sub - z) % n_tiles

    def gather(field):
        along = [field] + [shifted(field, "tiles", n_tiles, d) for d in range(1, n_tiles)]
        pieces = list(along)
        for e in range(1, n_sub):
            pieces += [shifted(piece, "sub", n_sub, e) for piece in along]
        return pieces

    pieces = gather(sources)
    numbers = jnp.stack([tile_rank, tile_row, tile_col])
    ins, outs, tables = [basis_in], [basis_out], [numbers]
    for d in range(1, n_rhs):
        tables.append(shifted(numbers, "rhs", n_rhs, d))
        ins.append(shifted(basis_in, "rhs", n_rhs, d))
        outs.append(shifted(basis_out, "rhs", n_rhs, d))
    ranks, block_rows, block_cols = jnp.concatenate(tables, axis=1)
    kept = lax.broadcasted_iota(jnp.int32, (ranks.shape[0], RMAX), 1) < ranks[:, None]
    rows_of = jnp.where(kept, target_slot(block_rows)[:, None], -1).reshape(1, -1)
    columns = jnp.broadcast_to(source_slot(block_cols)[:, None], kept.shape).reshape(1, -1)
    near_slots = source_slot(near_col[0])
    near_blocks = near_blocks[0]

    def apply_once(pieces):
        keep, send = far_field(pieces, ins, outs, columns, rows_of, n_tiles)
        total = keep.astype(F32)
        for e in range(1, n_sub):
            size = n_tiles * rows
            total += shifted(send[(e - 1) * size : e * size], "sub", n_sub, e).astype(F32)
        sums = []
        for d in range(n_tiles):
            part = total[d * rows : (d + 1) * rows].astype(BF16)
            sums.append(shifted(part, "tiles", n_tiles, d) if d else part)
        near = near_field(pieces, near_blocks, near_slots)
        return finish(sums, near, jacobi_inverse)

    first_result = apply_once(pieces)
    second_result = apply_once(gather(first_result))
    return (first_result, second_result)


def solution(mesh):
    sizes = mesh.shape
    return jax.shard_map(
        functools.partial(local, sizes["tiles"], sizes["rhs"], sizes["sub"]),
        mesh=mesh,
        in_specs=(
            P("rhs", ("groups", "tiles", "sub")),
            P(("groups", "tiles", "rhs", "sub"), None, None),
            P(("groups", "tiles", "rhs", "sub"), None, None),
            P(("groups", "tiles", "rhs", "sub")),
            P(("groups", "tiles", "rhs", "sub")),
            P(("groups", "tiles", "rhs", "sub")),
            P(("groups", "tiles", "sub"), None, None, None),
            P(("groups", "tiles", "sub"), None),
            P(("groups", "tiles", "sub"), None, None),
        ),
        out_specs=(P("rhs", ("groups", "tiles", "sub")), P("rhs", ("groups", "tiles", "sub"))),
        check_vma=False,
    )
```

```python
import functools

import jax
import jax.numpy as jnp
from jax import lax
from jax.experimental import pallas as pl
from jax.experimental.pallas import tpu as pltpu
from jax.sharding import PartitionSpec as P

BLK = 512
RMAX = 64
JB = 128
NCHUNK = 256
BF16 = jnp.bfloat16
F32 = jnp.float32
CONTRACT_LAST = (((1,), (1,)), ((), ()))


def shifted(value, axis, size, amount):
    return lax.ppermute(value, axis, [(i, (i + amount) % size) for i in range(size)])


def fetch(pieces, stacked, sems):
    rows = pieces[0].shape[0]
    copies = [
        pltpu.make_async_copy(piece, stacked.at[pl.ds(i * rows, rows)], sems.at[i])
        for i, piece in enumerate(pieces)
    ]
    for copy in copies:
        copy.start()
    for copy in copies:
        copy.wait()


def spread(values):
    tile = lax.broadcasted_iota(jnp.int32, (1, NCHUNK), 1) // RMAX
    out = jnp.full((1, NCHUNK), values[0], jnp.int32)
    for i, value in enumerate(values[1:], 1):
        out = jnp.where(tile == i, value, out)
    return out


def far_kernel(sizes, n_parts, has_partial, final, place_ref, *refs):
    n_tiles, n_sub = sizes
    n_pieces = n_tiles * n_sub
    tables, refs = refs[:n_parts], refs[n_parts:]
    pieces, refs = refs[:n_pieces], refs[n_pieces:]
    ins, refs = refs[:n_parts], refs[n_parts:]
    outs, refs = refs[:n_parts], refs[n_parts:]
    partial, refs = refs[:has_partial], refs[has_partial:]
    results, (stacked, masked, sems) = refs[:-3], refs[-3:]
    z, s = place_ref[0], place_ref[1]
    rows = pieces[0].shape[0]
    width = ins[0].shape[0]
    per_chunk = NCHUNK // RMAX
    fetch(pieces, stacked, sems)
    lane = lax.broadcasted_iota(jnp.int32, (1, NCHUNK), 1) % RMAX
    for part in range(n_parts):
        for chunk in range(width // NCHUNK):
            tiles = range(chunk * per_chunk, (chunk + 1) * per_chunk)
            ranks = spread([tables[part][0, t] for t in tiles])
            block_rows = [tables[part][1, t] for t in tiles]
            block_cols = [tables[part][2, t] for t in tiles]
            column = spread(
                [
                    lax.rem(s + n_sub - lax.rem(j, n_sub), n_sub) * n_tiles
                    + lax.rem(z + n_tiles - lax.div(j, n_sub), n_tiles)
                    for j in block_cols
                ]
            )
            target = spread(
                [
                    lax.rem(lax.rem(j, n_sub) + n_sub - s, n_sub) * n_tiles
                    + lax.rem(lax.div(j, n_sub) + n_tiles - z, n_tiles)
                    for j in block_rows
                ]
            )
            target = jnp.where(lane < ranks, target, -1)
            products = lax.dot_general(
                stacked[...],
                ins[part][chunk * NCHUNK : (chunk + 1) * NCHUNK, :],
                CONTRACT_LAST,
                preferred_element_type=F32,
            )
            chosen = products[:rows]
            for piece in range(1, n_pieces):
                chosen = jnp.where(
                    column == piece, products[piece * rows : (piece + 1) * rows], chosen
                )
            first = part * width + chunk * NCHUNK
            for piece in range(n_pieces):
                masked[piece * rows : (piece + 1) * rows, first : first + NCHUNK] = jnp.where(
                    target == piece, chosen, 0.0
                ).astype(BF16)
    total = partial[0][...] if has_partial else None
    for part in range(n_parts):
        added = jnp.dot(
            masked[:, part * width : (part + 1) * width],
            outs[part][...],
            preferred_element_type=F32,
        )
        total = added if total is None else total + added
    if final:
        keep_ref, send_ref = results
        total = total.astype(BF16)
        keep_ref[...] = total[: n_tiles * rows]
        send_ref[...] = total[n_tiles * rows :]
    else:
        results[0][...] = total


def far_field(sizes, place, tables, pieces, ins, outs, partial=None, final=True):
    rows = pieces[0].shape[0]
    n_pieces, n_parts, width = len(pieces), len(ins), ins[0].shape[0]
    n_keep = sizes[0]
    whole = pl.BlockSpec(memory_space=pltpu.VMEM)
    scalars = pl.BlockSpec(memory_space=pltpu.SMEM)
    anywhere = pl.BlockSpec(memory_space=pl.ANY)
    if final:
        out_shape = (
            jax.ShapeDtypeStruct((n_keep * rows, BLK), BF16),
            jax.ShapeDtypeStruct(((n_pieces - n_keep) * rows, BLK), BF16),
        )
    else:
        out_shape = (jax.ShapeDtypeStruct((n_pieces * rows, BLK), F32),)
    partials = [] if partial is None else [partial]
    limit = n_pieces * rows * (2 * BLK + 2 * n_parts * width + 16 * BLK + 4 * NCHUNK)
    limit += 4 * n_parts * width * BLK + (4 << 20)
    out = pl.pallas_call(
        functools.partial(far_kernel, sizes, n_parts, len(partials), final),
        out_shape=out_shape,
        in_specs=[scalars] * (1 + n_parts)
        + [anywhere] * n_pieces
        + [whole] * (2 * n_parts + len(partials)),
        out_specs=(whole,) * len(out_shape),
        scratch_shapes=[
            pltpu.VMEM((n_pieces * rows, BLK), BF16),
            pltpu.VMEM((n_pieces * rows, n_parts * width), BF16),
            pltpu.SemaphoreType.DMA((n_pieces,)),
        ],
        compiler_params=pltpu.CompilerParams(vmem_limit_bytes=limit),
        cost_estimate=pl.CostEstimate(
            flops=4 * n_pieces * rows * n_parts * width * BLK,
            transcendentals=0,
            bytes_accessed=2 * BLK * (2 * n_pieces * rows + 2 * n_parts * width),
        ),
        name="far_field",
    )(place, *tables, *pieces, *ins, *outs, *partials)
    return out if final else out[0]


def near_kernel(n_pieces, per_step, slot_ref, *refs):
    pieces = refs[:n_pieces]
    blocks_ref, out_ref, stacked, sems = refs[n_pieces:]
    rows = pieces[0].shape[0]
    step = pl.program_id(0)

    @pl.when(step == 0)
    def _():
        fetch(pieces, stacked, sems)
        out_ref[...] = jnp.zeros_like(out_ref)

    total = out_ref[...]
    for k in range(per_step):
        start = pl.multiple_of(slot_ref[step * per_step + k] * rows, rows)
        total += lax.dot_general(
            stacked[pl.ds(start, rows), :],
            blocks_ref[k],
            CONTRACT_LAST,
            preferred_element_type=F32,
        )
    out_ref[...] = total


def near_field(pieces, near_blocks, slots):
    rows = pieces[0].shape[0]
    n_pieces, near = len(pieces), near_blocks.shape[0]
    per_step = 4 if near % 4 == 0 else 1
    anywhere = pl.BlockSpec(memory_space=pl.ANY)
    return pl.pallas_call(
        functools.partial(near_kernel, n_pieces, per_step),
        out_shape=jax.ShapeDtypeStruct((rows, BLK), F32),
        grid_spec=pltpu.PrefetchScalarGridSpec(
            num_scalar_prefetch=1,
            grid=(near // per_step,),
            in_specs=[anywhere] * n_pieces
            + [pl.BlockSpec((per_step, BLK, BLK), lambda step, slot: (step, 0, 0))],
            out_specs=pl.BlockSpec((rows, BLK), lambda step, slot: (0, 0)),
            scratch_shapes=[
                pltpu.VMEM((n_pieces * rows, BLK), BF16),
                pltpu.SemaphoreType.DMA((n_pieces,)),
            ],
        ),
        compiler_params=pltpu.CompilerParams(vmem_limit_bytes=12 << 20),
        cost_estimate=pl.CostEstimate(
            flops=2 * near * rows * BLK * BLK,
            transcendentals=0,
            bytes_accessed=2 * BLK * (near * BLK + n_pieces * rows + 2 * rows),
        ),
        name="near_field",
    )(slots, *pieces, near_blocks)


def finish_kernel(n_sums, *refs):
    sums, (near_ref, jacobi_ref, out_ref) = refs[:n_sums], refs[n_sums:]
    total = near_ref[...]
    for part in sums:
        total += part[...].astype(F32)
    field = total.astype(BF16)
    for group in range(jacobi_ref.shape[0]):
        here = slice(group * JB, (group + 1) * JB)
        out_ref[:, here] = lax.dot_general(
            field[:, here], jacobi_ref[group], CONTRACT_LAST, preferred_element_type=F32
        ).astype(BF16)


def finish(sums, near, jacobi_inverse):
    whole = pl.BlockSpec(memory_space=pltpu.VMEM)
    return pl.pallas_call(
        functools.partial(finish_kernel, len(sums)),
        out_shape=jax.ShapeDtypeStruct(near.shape, BF16),
        in_specs=[whole] * (len(sums) + 2),
        out_specs=whole,
        compiler_params=pltpu.CompilerParams(vmem_limit_bytes=4 << 20),
        name="finish",
    )(*sums, near, jacobi_inverse)


def local(
    n_tiles,
    n_rhs,
    n_sub,
    sources,
    basis_out,
    basis_in,
    tile_rank,
    tile_row,
    tile_col,
    near_blocks,
    near_col,
    jacobi_inverse,
):
    z = lax.axis_index("tiles")
    s = lax.axis_index("sub")
    rows = sources.shape[0]
    basis_in = basis_in.reshape(-1, BLK)
    basis_out = basis_out.reshape(-1, BLK)

    def source_slot(block):
        return (s - block % n_sub) % n_sub * n_tiles + (z - block // n_sub) % n_tiles

    def gather(field):
        along = [field] + [shifted(field, "tiles", n_tiles, d) for d in range(1, n_tiles)]
        pieces = list(along)
        for e in range(1, n_sub):
            pieces += [shifted(piece, "sub", n_sub, e) for piece in along]
        return pieces

    pieces = gather(sources)
    numbers = jnp.stack([tile_rank, tile_row, tile_col])
    ins, outs, tables = [basis_in], [basis_out], [numbers]
    for d in range(1, n_rhs):
        tables.append(shifted(numbers, "rhs", n_rhs, d))
        ins.append(shifted(basis_in, "rhs", n_rhs, d))
        outs.append(shifted(basis_out, "rhs", n_rhs, d))
    sizes = (n_tiles, n_sub)
    place = jnp.stack([z, s])
    near_slots = source_slot(near_col[0])
    near_blocks = near_blocks[0]

    def reduce_and_finish(pieces, keep, send):
        total = keep.astype(F32)
        for e in range(1, n_sub):
            size = n_tiles * rows
            total += shifted(send[(e - 1) * size : e * size], "sub", n_sub, e).astype(F32)
        sums = []
        for d in range(n_tiles):
            part = total[d * rows : (d + 1) * rows].astype(BF16)
            sums.append(shifted(part, "tiles", n_tiles, d) if d else part)
        near = near_field(pieces, near_blocks, near_slots)
        return finish(sums, near, jacobi_inverse)

    partial = far_field(sizes, place, tables[:1], pieces, ins[:1], outs[:1], final=False)
    keep, send = far_field(sizes, place, tables[1:], pieces, ins[1:], outs[1:], partial=partial)
    first_result = reduce_and_finish(pieces, keep, send)
    pieces = gather(first_result)
    keep, send = far_field(sizes, place, tables, pieces, ins, outs)
    second_result = reduce_and_finish(pieces, keep, send)
    return (first_result, second_result)


def solution(mesh):
    sizes = mesh.shape
    return jax.shard_map(
        functools.partial(local, sizes["tiles"], sizes["rhs"], sizes["sub"]),
        mesh=mesh,
        in_specs=(
            P("rhs", ("groups", "tiles", "sub")),
            P(("groups", "tiles", "rhs", "sub"), None, None),
            P(("groups", "tiles", "rhs", "sub"), None, None),
            P(("groups", "tiles", "rhs", "sub")),
            P(("groups", "tiles", "rhs", "sub")),
            P(("groups", "tiles", "rhs", "sub")),
            P(("groups", "tiles", "sub"), None, None, None),
            P(("groups", "tiles", "sub"), None),
            P(("groups", "tiles", "sub"), None, None),
        ),
        out_specs=(P("rhs", ("groups", "tiles", "sub")), P("rhs", ("groups", "tiles", "sub"))),
        check_vma=False,
    )
```

```python
import functools

import jax
import jax.numpy as jnp
from jax import lax
from jax.experimental import pallas as pl
from jax.experimental.pallas import tpu as pltpu
from jax.sharding import PartitionSpec as P

BLK = 512
RMAX = 64
JB = 128
NCHUNK = 256
BF16 = jnp.bfloat16
F32 = jnp.float32
CONTRACT_LAST = (((1,), (1,)), ((), ()))


def shifted(value, axis, size, amount):
    return lax.ppermute(value, axis, [(i, (i + amount) % size) for i in range(size)])


def stack(pieces, stacked):
    rows = pieces[0].shape[0]
    for i, piece in enumerate(pieces):
        stacked[i * rows : (i + 1) * rows, :] = piece[...]


def spread(values):
    tile = lax.broadcasted_iota(jnp.int32, (1, NCHUNK), 1) // RMAX
    out = jnp.full((1, NCHUNK), values[0], jnp.int32)
    for i, value in enumerate(values[1:], 1):
        out = jnp.where(tile == i, value, out)
    return out


def far_kernel(sizes, n_parts, has_partial, final, place_ref, *refs):
    n_tiles, n_sub = sizes
    n_pieces = n_tiles * n_sub
    tables, refs = refs[:n_parts], refs[n_parts:]
    pieces, refs = refs[:n_pieces], refs[n_pieces:]
    ins, refs = refs[:n_parts], refs[n_parts:]
    outs, refs = refs[:n_parts], refs[n_parts:]
    partial, refs = refs[:has_partial], refs[has_partial:]
    results, (stacked, masked) = refs[:-2], refs[-2:]
    z, s = place_ref[0], place_ref[1]
    rows = pieces[0].shape[0]
    width = ins[0].shape[0]
    per_chunk = NCHUNK // RMAX
    stack(pieces, stacked)
    lane = lax.broadcasted_iota(jnp.int32, (1, NCHUNK), 1) % RMAX
    for part in range(n_parts):
        for chunk in range(width // NCHUNK):
            tiles = range(chunk * per_chunk, (chunk + 1) * per_chunk)
            ranks = spread([tables[part][0, t] for t in tiles])
            block_rows = [tables[part][1, t] for t in tiles]
            block_cols = [tables[part][2, t] for t in tiles]
            column = spread(
                [
                    lax.rem(s + n_sub - lax.rem(j, n_sub), n_sub) * n_tiles
                    + lax.rem(z + n_tiles - lax.div(j, n_sub), n_tiles)
                    for j in block_cols
                ]
            )
            target = spread(
                [
                    lax.rem(lax.rem(j, n_sub) + n_sub - s, n_sub) * n_tiles
                    + lax.rem(lax.div(j, n_sub) + n_tiles - z, n_tiles)
                    for j in block_rows
                ]
            )
            target = jnp.where(lane < ranks, target, -1)
            products = lax.dot_general(
                stacked[...],
                ins[part][chunk * NCHUNK : (chunk + 1) * NCHUNK, :],
                CONTRACT_LAST,
                preferred_element_type=F32,
            )
            chosen = products[:rows]
            for piece in range(1, n_pieces):
                chosen = jnp.where(
                    column == piece, products[piece * rows : (piece + 1) * rows], chosen
                )
            first = part * width + chunk * NCHUNK
            for piece in range(n_pieces):
                masked[piece * rows : (piece + 1) * rows, first : first + NCHUNK] = jnp.where(
                    target == piece, chosen, 0.0
                ).astype(BF16)
    total = partial[0][...] if has_partial else None
    for part in range(n_parts):
        added = jnp.dot(
            masked[:, part * width : (part + 1) * width],
            outs[part][...],
            preferred_element_type=F32,
        )
        total = added if total is None else total + added
    if final:
        keep_ref, send_ref = results
        total = total.astype(BF16)
        keep_ref[...] = total[: n_tiles * rows]
        send_ref[...] = total[n_tiles * rows :]
    else:
        results[0][...] = total


def far_field(sizes, place, parts, pieces, partial=None, final=True):
    tables, ins, outs = zip(*parts)
    rows = pieces[0].shape[0]
    n_pieces, n_parts, width = len(pieces), len(ins), ins[0].shape[0]
    n_keep = sizes[0]
    whole = pl.BlockSpec(memory_space=pltpu.VMEM)
    scalars = pl.BlockSpec(memory_space=pltpu.SMEM)
    if final:
        out_shape = (
            jax.ShapeDtypeStruct((n_keep * rows, BLK), BF16),
            jax.ShapeDtypeStruct(((n_pieces - n_keep) * rows, BLK), BF16),
        )
    else:
        out_shape = (jax.ShapeDtypeStruct((n_pieces * rows, BLK), F32),)
    partials = [] if partial is None else [partial]
    limit = n_pieces * rows * (2 * BLK + 2 * n_parts * width + 16 * BLK + 4 * NCHUNK)
    limit += 4 * n_parts * width * BLK + (4 << 20)
    out = pl.pallas_call(
        functools.partial(far_kernel, sizes, n_parts, len(partials), final),
        out_shape=out_shape,
        in_specs=[scalars] * (1 + n_parts)
        + [whole] * (n_pieces + 2 * n_parts + len(partials)),
        out_specs=(whole,) * len(out_shape),
        scratch_shapes=[
            pltpu.VMEM((n_pieces * rows, BLK), BF16),
            pltpu.VMEM((n_pieces * rows, n_parts * width), BF16),
        ],
        compiler_params=pltpu.CompilerParams(vmem_limit_bytes=limit),
        cost_estimate=pl.CostEstimate(
            flops=4 * n_pieces * rows * n_parts * width * BLK,
            transcendentals=0,
            bytes_accessed=2 * BLK * (2 * n_pieces * rows + 2 * n_parts * width),
        ),
        name="far_field",
    )(place, *tables, *pieces, *ins, *outs, *partials)
    return out if final else out[0]


def near_kernel(n_halves, n_pieces, per_step, slot_ref, *refs):
    pieces, (blocks_ref, *results, stacked, total) = (
        refs[: n_halves * n_pieces],
        refs[n_halves * n_pieces :],
    )
    rows = pieces[0].shape[0]
    step = pl.program_id(0)

    @pl.when(step == 0)
    def _():
        for half in range(n_halves):
            for i in range(n_pieces):
                stacked[i, half * rows : (half + 1) * rows, :] = pieces[half * n_pieces + i][...]
        total[...] = jnp.zeros_like(total)

    added = total[...]
    for k in range(per_step):
        added += lax.dot_general(
            stacked[slot_ref[step * per_step + k]],
            blocks_ref[k],
            CONTRACT_LAST,
            preferred_element_type=F32,
        )
    total[...] = added

    @pl.when(step == pl.num_programs(0) - 1)
    def _():
        for half, result in enumerate(results):
            result[...] = total[half * rows : (half + 1) * rows, :]


def near_field(halves, near_blocks, slots):
    rows = halves[0][0].shape[0]
    n_halves, n_pieces, near = len(halves), len(halves[0]), near_blocks.shape[0]
    per_step = 4 if near % 4 == 0 else 1
    whole = pl.BlockSpec(memory_space=pltpu.VMEM)
    return pl.pallas_call(
        functools.partial(near_kernel, n_halves, n_pieces, per_step),
        out_shape=(jax.ShapeDtypeStruct((rows, BLK), F32),) * n_halves,
        grid_spec=pltpu.PrefetchScalarGridSpec(
            num_scalar_prefetch=1,
            grid=(near // per_step,),
            in_specs=[whole] * (n_halves * n_pieces)
            + [pl.BlockSpec((per_step, BLK, BLK), lambda step, slot: (step, 0, 0))],
            out_specs=(whole,) * n_halves,
            scratch_shapes=[
                pltpu.VMEM((n_pieces, n_halves * rows, BLK), BF16),
                pltpu.VMEM((n_halves * rows, BLK), F32),
            ],
        ),
        compiler_params=pltpu.CompilerParams(vmem_limit_bytes=14 << 20),
        cost_estimate=pl.CostEstimate(
            flops=2 * near * n_halves * rows * BLK * BLK,
            transcendentals=0,
            bytes_accessed=2 * BLK * near * BLK,
        ),
        name="near_field",
    )(slots, *[piece for half in halves for piece in half], near_blocks)


def finish_kernel(n_sums, n_before, *refs):
    sums, (near_ref, jacobi_ref), refs = refs[:n_sums], refs[n_sums : n_sums + 2], refs[n_sums + 2 :]
    before, (field_ref, *results) = refs[:n_before], refs[n_before:]
    total = near_ref[...]
    for part in sums:
        total += part[...].astype(F32)
    rows = total.shape[0]
    field = total.astype(BF16)
    for group in range(jacobi_ref.shape[0]):
        here = slice(group * JB, (group + 1) * JB)
        field_ref[:, here] = lax.dot_general(
            field[:, here], jacobi_ref[group], CONTRACT_LAST, preferred_element_type=F32
        ).astype(BF16)
    for result in results:
        for i, ref in enumerate([*before, field_ref]):
            result[i * rows : (i + 1) * rows, :] = ref[...]


def finish(sums, near, jacobi_inverse, before=(), last=False):
    whole = pl.BlockSpec(memory_space=pltpu.VMEM)
    rows = near.shape[0]
    out_shape = [jax.ShapeDtypeStruct(near.shape, BF16)]
    if last:
        out_shape.append(jax.ShapeDtypeStruct(((len(before) + 1) * rows, BLK), BF16))
    return pl.pallas_call(
        functools.partial(finish_kernel, len(sums), len(before) if last else 0),
        out_shape=tuple(out_shape),
        in_specs=[whole] * (len(sums) + 2 + (len(before) if last else 0)),
        out_specs=(whole,) * len(out_shape),
        compiler_params=pltpu.CompilerParams(vmem_limit_bytes=4 << 20),
        name="finish",
    )(*sums, near, jacobi_inverse, *(before if last else ()))


def local(
    n_tiles,
    n_rhs,
    n_sub,
    sources,
    basis_out,
    basis_in,
    tile_rank,
    tile_row,
    tile_col,
    near_blocks,
    near_col,
    jacobi_inverse,
):
    z = lax.axis_index("tiles")
    s = lax.axis_index("sub")
    basis_in = basis_in.reshape(-1, BLK)
    basis_out = basis_out.reshape(-1, BLK)

    def source_slot(block):
        return (s - block % n_sub) % n_sub * n_tiles + (z - block // n_sub) % n_tiles

    def gather(field):
        along = [field] + [shifted(field, "tiles", n_tiles, d) for d in range(1, n_tiles)]
        pieces = list(along)
        for e in range(1, n_sub):
            pieces += [shifted(piece, "sub", n_sub, e) for piece in along]
        return pieces

    n_halves = 1
    rows = sources.shape[0] // n_halves
    numbers = jnp.stack([tile_rank, tile_row, tile_col])
    parts = [(numbers, basis_in, basis_out)]
    for e in range(1, n_rhs):
        parts.append(tuple(shifted(array, "rhs", n_rhs, e) for array in parts[0]))
    halves = [gather(sources[h * rows : (h + 1) * rows]) for h in range(n_halves)]
    sizes = (n_tiles, n_sub)
    place = jnp.stack([z, s])
    near_slots = source_slot(near_col[0])
    near_blocks = near_blocks[0]

    def exchange(keep, send):
        total = keep.astype(F32)
        for e in range(1, n_sub):
            size = n_tiles * rows
            total += shifted(send[(e - 1) * size : e * size], "sub", n_sub, e).astype(F32)
        sums = []
        for d in range(n_tiles):
            part = total[d * rows : (d + 1) * rows].astype(BF16)
            sums.append(shifted(part, "tiles", n_tiles, d) if d else part)
        return sums

    def finish_all(sums, nears):
        fields = []
        for h in range(n_halves):
            out = finish(sums[h], nears[h], jacobi_inverse, fields, h == n_halves - 1)
            fields.append(out[0])
        return fields, out[1]

    nears = near_field(halves, near_blocks, near_slots)
    partials = [far_field(sizes, place, parts[:1], half, final=False) for half in halves]
    sums = [
        exchange(*far_field(sizes, place, parts[1:], half, partial=partial))
        for half, partial in zip(halves, partials)
    ]
    fields, first_result = finish_all(sums, nears)
    halves = [gather(field) for field in fields]
    sums = [exchange(*far_field(sizes, place, parts, half)) for half in halves]
    nears = near_field(halves, near_blocks, near_slots)
    fields, second_result = finish_all(sums, nears)
    return (first_result, second_result)


def solution(mesh):
    sizes = mesh.shape
    return jax.shard_map(
        functools.partial(local, sizes["tiles"], sizes["rhs"], sizes["sub"]),
        mesh=mesh,
        in_specs=(
            P("rhs", ("groups", "tiles", "sub")),
            P(("groups", "tiles", "rhs", "sub"), None, None),
            P(("groups", "tiles", "rhs", "sub"), None, None),
            P(("groups", "tiles", "rhs", "sub")),
            P(("groups", "tiles", "rhs", "sub")),
            P(("groups", "tiles", "rhs", "sub")),
            P(("groups", "tiles", "sub"), None, None, None),
            P(("groups", "tiles", "sub"), None),
            P(("groups", "tiles", "sub"), None, None),
        ),
        out_specs=(P("rhs", ("groups", "tiles", "sub")), P("rhs", ("groups", "tiles", "sub"))),
        check_vma=False,
    )
```

```python
import functools

import jax
import jax.numpy as jnp
from jax import lax
from jax.experimental import pallas as pl
from jax.experimental.pallas import tpu as pltpu
from jax.sharding import PartitionSpec as P

BLK = 512
RMAX = 64
JOIN = 10
EARLY = 10
JB = 128
NCHUNK = 256
BF16 = jnp.bfloat16
F32 = jnp.float32


def hint(us):
    return pl.CostEstimate(flops=int(us * 1e9) + 1, transcendentals=0, bytes_accessed=1)


CONTRACT_LAST = (((1,), (1,)), ((), ()))


def shifted(value, axis, size, amount):
    return lax.ppermute(value, axis, [(i, (i + amount) % size) for i in range(size)])


def on_chip(kernel, scalars, arrays, out_shapes, scratch, cost, limit, name):
    scalars, scalar_tree = jax.tree.flatten(scalars)
    arrays, array_tree = jax.tree.flatten(arrays)
    n_scalars, n_in, n_out = len(scalars), len(arrays), len(out_shapes)
    whole = pl.BlockSpec(memory_space=pltpu.VMEM)
    in_smem = pl.BlockSpec(memory_space=pltpu.SMEM)

    def body(*refs):
        numbers = jax.tree.unflatten(scalar_tree, refs[:n_scalars])
        inputs = jax.tree.unflatten(array_tree, refs[n_scalars : n_scalars + n_in])
        rest = refs[n_scalars + n_in :]
        kernel(numbers, inputs, rest[:n_out], rest[n_out:])

    moved = sum(a.size * a.dtype.itemsize for a in [*arrays, *out_shapes])
    return pl.pallas_call(
        body,
        out_shape=tuple(out_shapes),
        in_specs=[in_smem] * n_scalars + [whole] * n_in,
        out_specs=(whole,) * n_out,
        scratch_shapes=scratch,
        compiler_params=pltpu.CompilerParams(vmem_limit_bytes=limit + moved),
        cost_estimate=hint(cost),
        name=name,
    )(*scalars, *arrays)


def stack(pieces, stacked):
    rows = pieces[0].shape[0]
    for i, piece in enumerate(pieces):
        stacked[i * rows : (i + 1) * rows, :] = piece[...]


def spread(values):
    tile = lax.broadcasted_iota(jnp.int32, (1, NCHUNK), 1) // RMAX
    out = jnp.full((1, NCHUNK), values[0], jnp.int32)
    for i, value in enumerate(values[1:], 1):
        out = jnp.where(tile == i, value, out)
    return out


def slots_of(place, table, tiles, sizes):
    n_tiles, n_sub = sizes
    z, s = place[0], place[1]
    lane = lax.broadcasted_iota(jnp.int32, (1, NCHUNK), 1) % RMAX
    column = spread(
        [
            lax.rem(s + n_sub - lax.rem(table[2, t], n_sub), n_sub) * n_tiles
            + lax.rem(z + n_tiles - lax.div(table[2, t], n_sub), n_tiles)
            for t in tiles
        ]
    )
    target = spread(
        [
            lax.rem(lax.rem(table[1, t], n_sub) + n_sub - s, n_sub) * n_tiles
            + lax.rem(lax.div(table[1, t], n_sub) + n_tiles - z, n_tiles)
            for t in tiles
        ]
    )
    return column, jnp.where(lane < spread([table[0, t] for t in tiles]), target, -1)


def first_stage(numbers, sizes, stacked, ins, lanes, previous, coeff, masked):
    place, tables = numbers
    n_pieces = sizes[0] * sizes[1]
    rows = stacked.shape[0] // n_pieces
    first = 0
    for table, basis in zip(tables, ins):
        for start in range(0, basis.shape[0], NCHUNK):
            tiles = range(start // RMAX, (start + NCHUNK) // RMAX)
            column, target = slots_of(place, table, tiles, sizes)
            products = lax.dot_general(
                stacked[...],
                basis[start : start + NCHUNK, lanes],
                CONTRACT_LAST,
                preferred_element_type=F32,
            )
            chosen = products[:rows]
            for piece in range(1, n_pieces):
                chosen = jnp.where(
                    column == piece, products[piece * rows : (piece + 1) * rows], chosen
                )
            there = slice(first, first + NCHUNK)
            if previous is not None:
                chosen = chosen + previous[:, there]
            if coeff is not None:
                coeff[:, there] = chosen
            if masked is not None:
                for piece in range(n_pieces):
                    masked[piece * rows : (piece + 1) * rows, there] = jnp.where(
                        target == piece, chosen, 0.0
                    ).astype(BF16)
            first += NCHUNK


def second_stage(masked, outs, lanes, total):
    first = 0
    for basis in outs:
        values = basis[...] if basis.shape[1] == lanes.stop - lanes.start else basis[:, lanes]
        added = jnp.dot(
            masked[:, first : first + basis.shape[0]], values, preferred_element_type=F32
        )
        total = added if total is None else total + added
        first += basis.shape[0]
    return total


def split_sums(total, keep_ref, send_ref, lanes):
    kept = keep_ref.shape[0]
    total = total.astype(BF16)
    keep_ref[:, lanes] = total[:kept]
    send_ref[:, lanes] = total[kept:]


def opening_kernel(sizes, numbers, inputs, results, scratch):
    pieces, ins, outs = inputs
    total, stacked = results
    (masked,) = scratch
    every = slice(0, BLK)
    stack(pieces, stacked)
    first_stage(numbers, sizes, stacked, ins, every, None, None, masked)
    total[...] = second_stage(masked, outs, every, None)


def masked_kernel(sizes, numbers, inputs, results, scratch):
    stacked, ins = inputs
    first_stage(numbers, sizes, stacked, ins, slice(0, BLK), None, None, results[0])


def joining_kernel(lanes, numbers, inputs, results, scratch):
    masked, partial, outs = inputs
    total = second_stage(masked, outs, lanes, partial[:, lanes])
    split_sums(total, *results, slice(0, lanes.stop - lanes.start))


def early_kernel(sizes, lanes, numbers, inputs, results, scratch):
    pieces, ins = inputs
    coeff, stacked = results
    stack(pieces, stacked)
    first_stage(numbers, sizes, stacked, ins, lanes, None, coeff, None)


def late_kernel(sizes, lanes, numbers, inputs, results, scratch):
    pieces, ins, previous, outs_by_lanes = inputs
    keep_ref, send_ref, stacked = results
    (masked,) = scratch
    stack(pieces, stacked)
    first_stage(numbers, sizes, stacked, ins, lanes[-1], previous, None, masked)
    for here, outs in zip(lanes, outs_by_lanes):
        split_sums(second_stage(masked, outs, here, None), keep_ref, send_ref, here)


def near_kernel(n_stacks, per_step, slot_ref, *refs):
    stacks, (blocks_ref, out_ref, *own, total) = refs[:n_stacks], refs[n_stacks:]
    rows = out_ref.shape[0]
    step = pl.program_id(0)

    @pl.when(step == 0)
    def _():
        total[...] = jnp.zeros_like(total)

    added = total[...]
    for k in range(per_step):
        start = pl.multiple_of(slot_ref[step * per_step + k] * rows, rows)
        first = 0
        for stacked in stacks:
            width = stacked.shape[1]
            added += lax.dot_general(
                stacked[pl.ds(start, rows), :],
                blocks_ref[k, :, first : first + width],
                CONTRACT_LAST,
                preferred_element_type=F32,
            )
            first += width
    total[...] = added

    @pl.when(step == pl.num_programs(0) - 1)
    def _():
        out_ref[...] = total[...]
        for ref in own:
            first = 0
            for stacked in stacks:
                ref[:, first : first + stacked.shape[1]] = stacked[:rows, :]
                first += stacked.shape[1]


def near_field(rows, stacks, near_blocks, slots, with_own):
    near = near_blocks.shape[0]
    per_step = 4 if near % 4 == 0 else 1
    whole = pl.BlockSpec(memory_space=pltpu.VMEM)
    out_shape = [jax.ShapeDtypeStruct((rows, BLK), F32)]
    if with_own:
        out_shape.append(jax.ShapeDtypeStruct((rows, BLK), BF16))
    return pl.pallas_call(
        functools.partial(near_kernel, len(stacks), per_step),
        out_shape=tuple(out_shape),
        grid_spec=pltpu.PrefetchScalarGridSpec(
            num_scalar_prefetch=1,
            grid=(near // per_step,),
            in_specs=[whole] * len(stacks)
            + [pl.BlockSpec((per_step, BLK, BLK), lambda step, slot: (step, 0, 0))],
            out_specs=(whole,) * len(out_shape),
            scratch_shapes=[pltpu.VMEM((rows, BLK), F32)],
        ),
        compiler_params=pltpu.CompilerParams(vmem_limit_bytes=14 << 20),
        cost_estimate=hint(0),
        name="near_field",
    )(slots, *stacks, near_blocks)


def finish_kernel(lanes, numbers, inputs, results, scratch):
    sums, near_ref, jacobi_ref = inputs
    total = near_ref[:, lanes]
    for part in sums:
        total += part[...].astype(F32)
    field = total.astype(BF16)
    for start in range(0, lanes.stop - lanes.start, JB):
        here = slice(start, start + JB)
        results[0][:, here] = lax.dot_general(
            field[:, here],
            jacobi_ref[(lanes.start + start) // JB],
            CONTRACT_LAST,
            preferred_element_type=F32,
        ).astype(BF16)


def finish(sums, near, jacobi_inverse, lanes):
    return on_chip(
        functools.partial(finish_kernel, lanes),
        (),
        (sums, near, jacobi_inverse),
        [jax.ShapeDtypeStruct(sums[0].shape, BF16)],
        [],
        0,
        2 << 20,
        "finish",
    )[0]


def local(
    n_tiles,
    n_rhs,
    n_sub,
    sources,
    basis_out,
    basis_in,
    tile_rank,
    tile_row,
    tile_col,
    near_blocks,
    near_col,
    jacobi_inverse,
):
    z = lax.axis_index("tiles")
    s = lax.axis_index("sub")
    rows = sources.shape[0]
    basis_in = basis_in.reshape(-1, BLK)
    basis_out = basis_out.reshape(-1, BLK)
    width = basis_in.shape[0]
    sizes = (n_tiles, n_sub)
    n_pieces = n_tiles * n_sub
    stack_rows = n_pieces * rows
    cuts = [slice(0, BLK // 2), slice(BLK // 2, BLK)]
    place = jnp.stack([z, s])
    near_slots = (s - near_col[0] % n_sub) % n_sub * n_tiles + (z - near_col[0] // n_sub) % n_tiles
    near_blocks = near_blocks[0]
    temporary = stack_rows * (16 * BLK + 8 * NCHUNK) + (2 << 20)

    def gather(field):
        along = [field] + [shifted(field, "tiles", n_tiles, d) for d in range(1, n_tiles)]
        pieces = list(along)
        for e in range(1, n_sub):
            pieces += [shifted(piece, "sub", n_sub, e) for piece in along]
        return pieces

    def others(array):
        return [shifted(array, "rhs", n_rhs, e) for e in range(1, n_rhs)]

    def reduced(keep, send):
        total = keep.astype(F32)
        for e in range(1, n_sub):
            size = n_tiles * rows
            total += shifted(send[(e - 1) * size : e * size], "sub", n_sub, e).astype(F32)
        return [total[d * rows : (d + 1) * rows].astype(BF16) for d in range(n_tiles)]

    def spread_out(parts):
        return [shifted(part, "tiles", n_tiles, d) if d else part for d, part in enumerate(parts)]

    def stacked_shape(lanes, dtype=BF16):
        return jax.ShapeDtypeStruct((stack_rows, lanes.stop - lanes.start), dtype)

    def split_shapes(columns):
        return [
            jax.ShapeDtypeStruct((n_tiles * rows, columns), BF16),
            jax.ShapeDtypeStruct((stack_rows - n_tiles * rows, columns), BF16),
        ]

    numbers = jnp.stack([tile_rank, tile_row, tile_col])
    other_tables = others(numbers)
    other_ins = others(basis_in)
    other_outs = [others(basis_out[:, lanes]) for lanes in cuts]
    every = slice(0, BLK)

    partial, stacked = on_chip(
        functools.partial(opening_kernel, sizes),
        (place, [numbers]),
        (gather(sources), [basis_in], [basis_out]),
        [stacked_shape(every, F32), stacked_shape(every)],
        [pltpu.VMEM((stack_rows, width), BF16)],
        0,
        temporary,
        "far_own",
    )
    (near,) = near_field(rows, [stacked], near_blocks, near_slots, False)
    stacked, near = lax.optimization_barrier((stacked, near))
    (masked,) = on_chip(
        functools.partial(masked_kernel, sizes),
        (place, other_tables),
        (stacked, other_ins),
        [jax.ShapeDtypeStruct((stack_rows, (n_rhs - 1) * width), BF16)],
        [],
        0,
        temporary,
        "far_first_stage",
    )
    fields, parts = [], ()
    for lanes, outs in zip(cuts, other_outs):
        if parts:
            fields.append(finish(spread_out(parts), near, jacobi_inverse, cuts[len(fields)]))
        keep, send = on_chip(
            functools.partial(joining_kernel, lanes),
            (),
            (masked, partial, outs),
            split_shapes(lanes.stop - lanes.start),
            [],
            JOIN if parts else 0,
            temporary,
            "far_second_stage",
        )
        parts = reduced(keep, send)
    fields.append(finish(spread_out(parts), near, jacobi_inverse, cuts[-1]))

    tables = (place, [numbers] + other_tables)
    ins = [basis_in] + other_ins
    coeff, first_stack = on_chip(
        functools.partial(early_kernel, sizes, cuts[0]),
        tables,
        (gather(fields[0]), ins),
        [jax.ShapeDtypeStruct((rows, n_rhs * width), F32), stacked_shape(cuts[0])],
        [],
        EARLY,
        temporary,
        "far_early",
    )
    keep, send, second_stack = on_chip(
        functools.partial(late_kernel, sizes, cuts),
        tables,
        (gather(fields[1]), ins, coeff, [[basis_out] + outs for outs in other_outs]),
        split_shapes(BLK) + [stacked_shape(cuts[1])],
        [pltpu.VMEM((stack_rows, n_rhs * width), BF16)],
        0,
        temporary,
        "far_late",
    )
    near, first_result = near_field(
        rows, [first_stack, second_stack], near_blocks, near_slots, True
    )
    second_result = finish(spread_out(reduced(keep, send)), near, jacobi_inverse, every)
    return (first_result, second_result)


def solution(mesh):
    sizes = mesh.shape
    return jax.shard_map(
        functools.partial(local, sizes["tiles"], sizes["rhs"], sizes["sub"]),
        mesh=mesh,
        in_specs=(
            P("rhs", ("groups", "tiles", "sub")),
            P(("groups", "tiles", "rhs", "sub"), None, None),
            P(("groups", "tiles", "rhs", "sub"), None, None),
            P(("groups", "tiles", "rhs", "sub")),
            P(("groups", "tiles", "rhs", "sub")),
            P(("groups", "tiles", "rhs", "sub")),
            P(("groups", "tiles", "sub"), None, None, None),
            P(("groups", "tiles", "sub"), None),
            P(("groups", "tiles", "sub"), None, None),
        ),
        out_specs=(P("rhs", ("groups", "tiles", "sub")), P("rhs", ("groups", "tiles", "sub"))),
        check_vma=False,
    )
```

```python
import functools

import jax
import jax.numpy as jnp
from jax import lax
from jax.experimental import pallas as pl
from jax.experimental.pallas import tpu as pltpu
from jax.sharding import PartitionSpec as P

BLK = 512
RMAX = 64
JOIN = 10
KEPT = 10
JB = 128
NCHUNK = 256
BF16 = jnp.bfloat16
F32 = jnp.float32


def hint(us):
    return pl.CostEstimate(flops=int(us * 1e9) + 1, transcendentals=0, bytes_accessed=1)


CONTRACT_LAST = (((1,), (1,)), ((), ()))


def shifted(value, axis, size, amount):
    return lax.ppermute(value, axis, [(i, (i + amount) % size) for i in range(size)])


def on_chip(kernel, scalars, arrays, out_shapes, scratch, cost, limit, name):
    scalars, scalar_tree = jax.tree.flatten(scalars)
    arrays, array_tree = jax.tree.flatten(arrays)
    n_scalars, n_in, n_out = len(scalars), len(arrays), len(out_shapes)
    whole = pl.BlockSpec(memory_space=pltpu.VMEM)
    in_smem = pl.BlockSpec(memory_space=pltpu.SMEM)

    def body(*refs):
        numbers = jax.tree.unflatten(scalar_tree, refs[:n_scalars])
        inputs = jax.tree.unflatten(array_tree, refs[n_scalars : n_scalars + n_in])
        rest = refs[n_scalars + n_in :]
        kernel(numbers, inputs, rest[:n_out], rest[n_out:])

    moved = sum(a.size * a.dtype.itemsize for a in [*arrays, *out_shapes])
    return pl.pallas_call(
        body,
        out_shape=tuple(out_shapes),
        in_specs=[in_smem] * n_scalars + [whole] * n_in,
        out_specs=(whole,) * n_out,
        scratch_shapes=scratch,
        compiler_params=pltpu.CompilerParams(vmem_limit_bytes=limit + moved),
        cost_estimate=hint(cost),
        name=name,
    )(*scalars, *arrays)


def stack(pieces, stacked):
    rows = pieces[0].shape[0]
    for i, piece in enumerate(pieces):
        stacked[i * rows : (i + 1) * rows, :] = piece[...]


def spread(values):
    tile = lax.broadcasted_iota(jnp.int32, (1, NCHUNK), 1) // RMAX
    out = jnp.full((1, NCHUNK), values[0], jnp.int32)
    for i, value in enumerate(values[1:], 1):
        out = jnp.where(tile == i, value, out)
    return out


def slots_of(place, table, tiles, sizes):
    n_tiles, n_sub = sizes
    z, s = place[0], place[1]
    lane = lax.broadcasted_iota(jnp.int32, (1, NCHUNK), 1) % RMAX
    column = spread(
        [
            lax.rem(s + n_sub - lax.rem(table[2, t], n_sub), n_sub) * n_tiles
            + lax.rem(z + n_tiles - lax.div(table[2, t], n_sub), n_tiles)
            for t in tiles
        ]
    )
    target = spread(
        [
            lax.rem(lax.rem(table[1, t], n_sub) + n_sub - s, n_sub) * n_tiles
            + lax.rem(lax.div(table[1, t], n_sub) + n_tiles - z, n_tiles)
            for t in tiles
        ]
    )
    return column, jnp.where(lane < spread([table[0, t] for t in tiles]), target, -1)


def first_stage(numbers, sizes, stacked, ins, lanes, previous, coeff, masked):
    place, tables = numbers
    n_pieces = sizes[0] * sizes[1]
    rows = stacked.shape[0] // n_pieces
    first = 0
    for table, basis in zip(tables, ins):
        for start in range(0, basis.shape[0], NCHUNK):
            tiles = range(start // RMAX, (start + NCHUNK) // RMAX)
            column, target = slots_of(place, table, tiles, sizes)
            products = lax.dot_general(
                stacked[...],
                basis[start : start + NCHUNK, lanes],
                CONTRACT_LAST,
                preferred_element_type=F32,
            )
            chosen = products[:rows]
            for piece in range(1, n_pieces):
                chosen = jnp.where(
                    column == piece, products[piece * rows : (piece + 1) * rows], chosen
                )
            there = slice(first, first + NCHUNK)
            if previous is not None:
                chosen = chosen + previous[:, there]
            if coeff is not None:
                coeff[:, there] = chosen
            if masked is not None:
                for piece in range(n_pieces):
                    masked[piece * rows : (piece + 1) * rows, there] = jnp.where(
                        target == piece, chosen, 0.0
                    ).astype(BF16)
            first += NCHUNK


def second_stage(masked, outs, lanes, total):
    first = 0
    for basis in outs:
        values = basis[...] if basis.shape[1] == lanes.stop - lanes.start else basis[:, lanes]
        added = jnp.dot(
            masked[:, first : first + basis.shape[0]], values, preferred_element_type=F32
        )
        total = added if total is None else total + added
        first += basis.shape[0]
    return total


def split_sums(total, keep_ref, send_ref, lanes):
    kept = keep_ref.shape[0]
    total = total.astype(BF16)
    keep_ref[:, lanes] = total[:kept]
    send_ref[:, lanes] = total[kept:]


def opening_kernel(sizes, numbers, inputs, results, scratch):
    pieces, ins, outs = inputs
    total, stacked = results
    (masked,) = scratch
    every = slice(0, BLK)
    stack(pieces, stacked)
    first_stage(numbers, sizes, stacked, ins, every, None, None, masked)
    total[...] = second_stage(masked, outs, every, None)


def masked_kernel(sizes, numbers, inputs, results, scratch):
    stacked, ins = inputs
    first_stage(numbers, sizes, stacked, ins, slice(0, BLK), None, None, results[0])


def joining_kernel(lanes, numbers, inputs, results, scratch):
    masked, partial, outs = inputs
    total = second_stage(masked, outs, lanes, partial[:, lanes])
    split_sums(total, *results, slice(0, lanes.stop - lanes.start))


def sent_kernel(sizes, lanes, numbers, inputs, results, scratch):
    pieces_by_lanes, ins, outs_by_lanes = inputs
    send_ref, stacked, kept = results
    (masked,) = scratch
    for here, pieces in zip(lanes, pieces_by_lanes):
        stack(pieces, stacked.at[:, here])
    first_stage(numbers, sizes, stacked, ins, slice(0, BLK), None, None, masked)
    n_kept = kept.shape[0]
    for here, outs in zip(lanes, outs_by_lanes):
        total = second_stage(masked.at[n_kept:, :], outs, here, None)
        send_ref[:, here] = total.astype(BF16)
    kept[...] = masked[:n_kept, :]


def kept_kernel(lanes, numbers, inputs, results, scratch):
    masked, outs_by_lanes = inputs
    for here, outs in zip(lanes, outs_by_lanes):
        results[0][:, here] = second_stage(masked, outs, here, None).astype(BF16)


def near_kernel(n_stacks, per_step, slot_ref, *refs):
    stacks, (blocks_ref, out_ref, *own, total) = refs[:n_stacks], refs[n_stacks:]
    rows = out_ref.shape[0]
    step = pl.program_id(0)

    @pl.when(step == 0)
    def _():
        total[...] = jnp.zeros_like(total)

    added = total[...]
    for k in range(per_step):
        start = pl.multiple_of(slot_ref[step * per_step + k] * rows, rows)
        first = 0
        for stacked in stacks:
            width = stacked.shape[1]
            added += lax.dot_general(
                stacked[pl.ds(start, rows), :],
                blocks_ref[k, :, first : first + width],
                CONTRACT_LAST,
                preferred_element_type=F32,
            )
            first += width
    total[...] = added

    @pl.when(step == pl.num_programs(0) - 1)
    def _():
        out_ref[...] = total[...]
        for ref in own:
            first = 0
            for stacked in stacks:
                ref[:, first : first + stacked.shape[1]] = stacked[:rows, :]
                first += stacked.shape[1]


def near_field(rows, stacks, near_blocks, slots, with_own):
    near = near_blocks.shape[0]
    per_step = 4 if near % 4 == 0 else 1
    whole = pl.BlockSpec(memory_space=pltpu.VMEM)
    out_shape = [jax.ShapeDtypeStruct((rows, BLK), F32)]
    if with_own:
        out_shape.append(jax.ShapeDtypeStruct((rows, BLK), BF16))
    return pl.pallas_call(
        functools.partial(near_kernel, len(stacks), per_step),
        out_shape=tuple(out_shape),
        grid_spec=pltpu.PrefetchScalarGridSpec(
            num_scalar_prefetch=1,
            grid=(near // per_step,),
            in_specs=[whole] * len(stacks)
            + [pl.BlockSpec((per_step, BLK, BLK), lambda step, slot: (step, 0, 0))],
            out_specs=(whole,) * len(out_shape),
            scratch_shapes=[pltpu.VMEM((rows, BLK), F32)],
        ),
        compiler_params=pltpu.CompilerParams(vmem_limit_bytes=14 << 20),
        cost_estimate=hint(0),
        name="near_field",
    )(slots, *stacks, near_blocks)


def finish_kernel(lanes, numbers, inputs, results, scratch):
    sums, near_ref, jacobi_ref = inputs
    total = near_ref[:, lanes]
    for part in sums:
        total += part[...].astype(F32)
    field = total.astype(BF16)
    for start in range(0, lanes.stop - lanes.start, JB):
        here = slice(start, start + JB)
        results[0][:, here] = lax.dot_general(
            field[:, here],
            jacobi_ref[(lanes.start + start) // JB],
            CONTRACT_LAST,
            preferred_element_type=F32,
        ).astype(BF16)


def finish(sums, near, jacobi_inverse, lanes):
    return on_chip(
        functools.partial(finish_kernel, lanes),
        (),
        (sums, near, jacobi_inverse),
        [jax.ShapeDtypeStruct(sums[0].shape, BF16)],
        [],
        0,
        2 << 20,
        "finish",
    )[0]


def local(
    n_tiles,
    n_rhs,
    n_sub,
    sources,
    basis_out,
    basis_in,
    tile_rank,
    tile_row,
    tile_col,
    near_blocks,
    near_col,
    jacobi_inverse,
):
    z = lax.axis_index("tiles")
    s = lax.axis_index("sub")
    rows = sources.shape[0]
    basis_in = basis_in.reshape(-1, BLK)
    basis_out = basis_out.reshape(-1, BLK)
    width = basis_in.shape[0]
    sizes = (n_tiles, n_sub)
    n_pieces = n_tiles * n_sub
    stack_rows = n_pieces * rows
    cuts = [slice(0, BLK // 2), slice(BLK // 2, BLK)]
    place = jnp.stack([z, s])
    near_slots = (s - near_col[0] % n_sub) % n_sub * n_tiles + (z - near_col[0] // n_sub) % n_tiles
    near_blocks = near_blocks[0]
    temporary = stack_rows * (16 * BLK + 8 * NCHUNK) + (2 << 20)

    def gather(field):
        along = [field] + [shifted(field, "tiles", n_tiles, d) for d in range(1, n_tiles)]
        pieces = list(along)
        for e in range(1, n_sub):
            pieces += [shifted(piece, "sub", n_sub, e) for piece in along]
        return pieces

    def others(array):
        return [shifted(array, "rhs", n_rhs, e) for e in range(1, n_rhs)]

    def reduced(keep, send):
        total = keep.astype(F32)
        for e in range(1, n_sub):
            size = n_tiles * rows
            total += shifted(send[(e - 1) * size : e * size], "sub", n_sub, e).astype(F32)
        return [total[d * rows : (d + 1) * rows].astype(BF16) for d in range(n_tiles)]

    def spread_out(parts):
        return [shifted(part, "tiles", n_tiles, d) if d else part for d, part in enumerate(parts)]

    def stacked_shape(lanes, dtype=BF16):
        return jax.ShapeDtypeStruct((stack_rows, lanes.stop - lanes.start), dtype)

    def split_shapes(columns):
        return [
            jax.ShapeDtypeStruct((n_tiles * rows, columns), BF16),
            jax.ShapeDtypeStruct((stack_rows - n_tiles * rows, columns), BF16),
        ]

    numbers = jnp.stack([tile_rank, tile_row, tile_col])
    other_tables = others(numbers)
    other_ins = others(basis_in)
    other_outs = [others(basis_out[:, lanes]) for lanes in cuts]
    every = slice(0, BLK)

    partial, stacked = on_chip(
        functools.partial(opening_kernel, sizes),
        (place, [numbers]),
        (gather(sources), [basis_in], [basis_out]),
        [stacked_shape(every, F32), stacked_shape(every)],
        [pltpu.VMEM((stack_rows, width), BF16)],
        0,
        temporary,
        "far_own",
    )
    (near,) = near_field(rows, [stacked], near_blocks, near_slots, False)
    stacked, near = lax.optimization_barrier((stacked, near))
    (masked,) = on_chip(
        functools.partial(masked_kernel, sizes),
        (place, other_tables),
        (stacked, other_ins),
        [jax.ShapeDtypeStruct((stack_rows, (n_rhs - 1) * width), BF16)],
        [],
        0,
        temporary,
        "far_first_stage",
    )
    fields, parts = [], ()
    for lanes, outs in zip(cuts, other_outs):
        if parts:
            fields.append(finish(spread_out(parts), near, jacobi_inverse, cuts[len(fields)]))
        keep, send = on_chip(
            functools.partial(joining_kernel, lanes),
            (),
            (masked, partial, outs),
            split_shapes(lanes.stop - lanes.start),
            [],
            JOIN if parts else 0,
            temporary,
            "far_second_stage",
        )
        parts = reduced(keep, send)
    fields.append(finish(spread_out(parts), near, jacobi_inverse, cuts[-1]))

    tables = (place, [numbers] + other_tables)
    ins = [basis_in] + other_ins
    outs = [[basis_out] + arrays for arrays in other_outs]
    keep_shape, send_shape = split_shapes(BLK)
    send, stacked, kept = on_chip(
        functools.partial(sent_kernel, sizes, cuts),
        tables,
        ([gather(field) for field in fields], ins, outs),
        [send_shape, stacked_shape(every)]
        + [jax.ShapeDtypeStruct((n_tiles * rows, n_rhs * width), BF16)],
        [pltpu.VMEM((stack_rows, n_rhs * width), BF16)],
        0,
        temporary,
        "far_sent",
    )
    (keep,) = on_chip(
        functools.partial(kept_kernel, cuts),
        (),
        (kept, outs),
        [keep_shape],
        [],
        KEPT,
        temporary,
        "far_kept",
    )
    near, first_result = near_field(rows, [stacked], near_blocks, near_slots, True)
    second_result = finish(spread_out(reduced(keep, send)), near, jacobi_inverse, every)
    return (first_result, second_result)


def solution(mesh):
    sizes = mesh.shape
    return jax.shard_map(
        functools.partial(local, sizes["tiles"], sizes["rhs"], sizes["sub"]),
        mesh=mesh,
        in_specs=(
            P("rhs", ("groups", "tiles", "sub")),
            P(("groups", "tiles", "rhs", "sub"), None, None),
            P(("groups", "tiles", "rhs", "sub"), None, None),
            P(("groups", "tiles", "rhs", "sub")),
            P(("groups", "tiles", "rhs", "sub")),
            P(("groups", "tiles", "rhs", "sub")),
            P(("groups", "tiles", "sub"), None, None, None),
            P(("groups", "tiles", "sub"), None),
            P(("groups", "tiles", "sub"), None, None),
        ),
        out_specs=(P("rhs", ("groups", "tiles", "sub")), P("rhs", ("groups", "tiles", "sub"))),
        check_vma=False,
    )
```

```python
import functools

import jax
import jax.numpy as jnp
from jax import lax
from jax.experimental import pallas as pl
from jax.experimental.pallas import tpu as pltpu
from jax.sharding import PartitionSpec as P

BLK = 512
RMAX = 64
JOIN = 10
KEPT = 10
JB = 128
NCHUNK = 256
BF16 = jnp.bfloat16
F32 = jnp.float32


def hint(us):
    return pl.CostEstimate(flops=int(us * 1e9) + 1, transcendentals=0, bytes_accessed=1)


CONTRACT_LAST = (((1,), (1,)), ((), ()))


def shifted(value, axis, size, amount):
    return lax.ppermute(value, axis, [(i, (i + amount) % size) for i in range(size)])


def on_chip(kernel, scalars, arrays, out_shapes, scratch, cost, limit, name):
    scalars, scalar_tree = jax.tree.flatten(scalars)
    arrays, array_tree = jax.tree.flatten(arrays)
    n_scalars, n_in, n_out = len(scalars), len(arrays), len(out_shapes)
    whole = pl.BlockSpec(memory_space=pltpu.VMEM)
    in_smem = pl.BlockSpec(memory_space=pltpu.SMEM)

    def body(*refs):
        numbers = jax.tree.unflatten(scalar_tree, refs[:n_scalars])
        inputs = jax.tree.unflatten(array_tree, refs[n_scalars : n_scalars + n_in])
        rest = refs[n_scalars + n_in :]
        kernel(numbers, inputs, rest[:n_out], rest[n_out:])

    moved = sum(a.size * a.dtype.itemsize for a in [*arrays, *out_shapes])
    return pl.pallas_call(
        body,
        out_shape=tuple(out_shapes),
        in_specs=[in_smem] * n_scalars + [whole] * n_in,
        out_specs=(whole,) * n_out,
        scratch_shapes=scratch,
        compiler_params=pltpu.CompilerParams(vmem_limit_bytes=limit + moved),
        cost_estimate=hint(cost),
        name=name,
    )(*scalars, *arrays)


def stack(pieces, stacked):
    rows = pieces[0].shape[0]
    for i, piece in enumerate(pieces):
        stacked[i * rows : (i + 1) * rows, :] = piece[...]


def spread(values):
    tile = lax.broadcasted_iota(jnp.int32, (1, NCHUNK), 1) // RMAX
    out = jnp.full((1, NCHUNK), values[0], jnp.int32)
    for i, value in enumerate(values[1:], 1):
        out = jnp.where(tile == i, value, out)
    return out


def slots_of(place, table, tiles, sizes):
    n_tiles, n_sub = sizes
    z, s = place[0], place[1]
    lane = lax.broadcasted_iota(jnp.int32, (1, NCHUNK), 1) % RMAX
    column = spread(
        [
            lax.rem(s + n_sub - lax.rem(table[2, t], n_sub), n_sub) * n_tiles
            + lax.rem(z + n_tiles - lax.div(table[2, t], n_sub), n_tiles)
            for t in tiles
        ]
    )
    target = spread(
        [
            lax.rem(lax.rem(table[1, t], n_sub) + n_sub - s, n_sub) * n_tiles
            + lax.rem(lax.div(table[1, t], n_sub) + n_tiles - z, n_tiles)
            for t in tiles
        ]
    )
    return column, jnp.where(lane < spread([table[0, t] for t in tiles]), target, -1)


def first_stage(numbers, sizes, stacked, ins, lanes, previous, coeff, masked):
    place, tables = numbers
    n_tiles, n_sub = sizes
    rows = stacked.shape[0] // (n_tiles * n_sub)
    first = 0
    for table, basis in zip(tables, ins):
        for start in range(0, basis.shape[0], NCHUNK):
            tiles = range(start // RMAX, (start + NCHUNK) // RMAX)
            target = slots_of(place, table, tiles, sizes)[1]
            found = []
            for t in tiles:
                block = table[2, t]
                slot = lax.rem(place[1] + n_sub - lax.rem(block, n_sub), n_sub) * n_tiles
                slot += lax.rem(place[0] + n_tiles - lax.div(block, n_sub), n_tiles)
                begin = pl.multiple_of(slot * rows, rows)
                found.append(
                    lax.dot_general(
                        stacked[pl.ds(begin, rows), :],
                        basis[t * RMAX : (t + 1) * RMAX, :],
                        CONTRACT_LAST,
                        preferred_element_type=F32,
                    )
                )
            chosen = jnp.concatenate(found, axis=1)
            there = slice(first, first + NCHUNK)
            for i, part in enumerate(masked):
                held = part.shape[0] // rows
                for piece in range(held):
                    part[piece * rows : (piece + 1) * rows, there] = jnp.where(
                        target == i * held + piece, chosen, 0.0
                    ).astype(BF16)
            first += NCHUNK


def second_stage(masked, outs, lanes, total):
    first = 0
    for basis in outs:
        values = basis[...] if basis.shape[1] == lanes.stop - lanes.start else basis[:, lanes]
        added = jnp.dot(
            masked[:, first : first + basis.shape[0]], values, preferred_element_type=F32
        )
        total = added if total is None else total + added
        first += basis.shape[0]
    return total


def split_sums(total, keep_ref, send_ref, lanes):
    kept = keep_ref.shape[0]
    total = total.astype(BF16)
    keep_ref[:, lanes] = total[:kept]
    send_ref[:, lanes] = total[kept:]


def opening_kernel(sizes, numbers, inputs, results, scratch):
    pieces, ins, outs = inputs
    total, stacked = results
    (masked,) = scratch
    every = slice(0, BLK)
    stack(pieces, stacked)
    first_stage(numbers, sizes, stacked, ins, every, None, None, [masked])
    total[...] = second_stage(masked, outs, every, None)


def masked_kernel(sizes, numbers, inputs, results, scratch):
    stacked, ins = inputs
    first_stage(numbers, sizes, stacked, ins, slice(0, BLK), None, None, results)


def joining_kernel(lanes, numbers, inputs, results, scratch):
    masked, partial, outs = inputs
    total = second_stage(masked, outs, lanes, partial[:, lanes])
    split_sums(total, *results, slice(0, lanes.stop - lanes.start))


def sent_kernel(sizes, lanes, numbers, inputs, results, scratch):
    pieces_by_lanes, ins, outs_by_lanes = inputs
    send_ref, stacked, *masked = results
    for here, pieces in zip(lanes, pieces_by_lanes):
        stack(pieces, stacked.at[:, here])
    first_stage(numbers, sizes, stacked, ins, slice(0, BLK), None, None, [*masked, *scratch])
    size = masked[0].shape[0]
    for here, outs in zip(lanes, outs_by_lanes):
        for i, part in enumerate(scratch):
            total = second_stage(part, outs, here, None)
            send_ref[i * size : (i + 1) * size, here] = total.astype(BF16)


def kept_kernel(lanes, numbers, inputs, results, scratch):
    masked, outs_by_lanes = inputs
    for here, outs in zip(lanes, outs_by_lanes):
        results[0][:, here] = second_stage(masked, outs, here, None).astype(BF16)


def near_kernel(n_stacks, per_step, slot_ref, *refs):
    stacks, (blocks_ref, out_ref, *own, total) = refs[:n_stacks], refs[n_stacks:]
    rows = out_ref.shape[0]
    step = pl.program_id(0)

    @pl.when(step == 0)
    def _():
        total[...] = jnp.zeros_like(total)

    added = total[...]
    for k in range(per_step):
        start = pl.multiple_of(slot_ref[step * per_step + k] * rows, rows)
        first = 0
        for stacked in stacks:
            width = stacked.shape[1]
            added += lax.dot_general(
                stacked[pl.ds(start, rows), :],
                blocks_ref[k, :, first : first + width],
                CONTRACT_LAST,
                preferred_element_type=F32,
            )
            first += width
    total[...] = added

    @pl.when(step == pl.num_programs(0) - 1)
    def _():
        out_ref[...] = total[...]
        for ref in own:
            first = 0
            for stacked in stacks:
                ref[:, first : first + stacked.shape[1]] = stacked[:rows, :]
                first += stacked.shape[1]


def near_field(rows, stacks, near_blocks, slots, with_own):
    near = near_blocks.shape[0]
    per_step = 4 if near % 4 == 0 else 1
    whole = pl.BlockSpec(memory_space=pltpu.VMEM)
    out_shape = [jax.ShapeDtypeStruct((rows, BLK), F32)]
    if with_own:
        out_shape.append(jax.ShapeDtypeStruct((rows, BLK), BF16))
    return pl.pallas_call(
        functools.partial(near_kernel, len(stacks), per_step),
        out_shape=tuple(out_shape),
        grid_spec=pltpu.PrefetchScalarGridSpec(
            num_scalar_prefetch=1,
            grid=(near // per_step,),
            in_specs=[whole] * len(stacks)
            + [pl.BlockSpec((per_step, BLK, BLK), lambda step, slot: (step, 0, 0))],
            out_specs=(whole,) * len(out_shape),
            scratch_shapes=[pltpu.VMEM((rows, BLK), F32)],
        ),
        compiler_params=pltpu.CompilerParams(vmem_limit_bytes=14 << 20),
        cost_estimate=hint(0),
        name="near_field",
    )(slots, *stacks, near_blocks)


def finish_kernel(lanes, numbers, inputs, results, scratch):
    sums, near_ref, jacobi_ref = inputs
    total = near_ref[:, lanes]
    for part in sums:
        total += part[...].astype(F32)
    field = total.astype(BF16)
    for start in range(0, lanes.stop - lanes.start, JB):
        here = slice(start, start + JB)
        results[0][:, here] = lax.dot_general(
            field[:, here],
            jacobi_ref[(lanes.start + start) // JB],
            CONTRACT_LAST,
            preferred_element_type=F32,
        ).astype(BF16)


def finish(sums, near, jacobi_inverse, lanes):
    return on_chip(
        functools.partial(finish_kernel, lanes),
        (),
        (sums, near, jacobi_inverse),
        [jax.ShapeDtypeStruct(sums[0].shape, BF16)],
        [],
        0,
        2 << 20,
        "finish",
    )[0]


def local(
    n_tiles,
    n_rhs,
    n_sub,
    sources,
    basis_out,
    basis_in,
    tile_rank,
    tile_row,
    tile_col,
    near_blocks,
    near_col,
    jacobi_inverse,
):
    z = lax.axis_index("tiles")
    s = lax.axis_index("sub")
    rows = sources.shape[0]
    basis_in = basis_in.reshape(-1, BLK)
    basis_out = basis_out.reshape(-1, BLK)
    width = basis_in.shape[0]
    sizes = (n_tiles, n_sub)
    n_pieces = n_tiles * n_sub
    stack_rows = n_pieces * rows
    cuts = [slice(0, BLK // 2), slice(BLK // 2, BLK)]
    place = jnp.stack([z, s])
    near_slots = (s - near_col[0] % n_sub) % n_sub * n_tiles + (z - near_col[0] // n_sub) % n_tiles
    near_blocks = near_blocks[0]
    temporary = stack_rows * (16 * BLK + 8 * NCHUNK) + (2 << 20)

    def gather(field):
        along = [field] + [shifted(field, "tiles", n_tiles, d) for d in range(1, n_tiles)]
        pieces = list(along)
        for e in range(1, n_sub):
            pieces += [shifted(piece, "sub", n_sub, e) for piece in along]
        return pieces

    def others(array):
        return [shifted(array, "rhs", n_rhs, e) for e in range(1, n_rhs)]

    def reduced(keep, send):
        total = keep.astype(F32)
        for e in range(1, n_sub):
            size = n_tiles * rows
            total += shifted(send[(e - 1) * size : e * size], "sub", n_sub, e).astype(F32)
        return [total[d * rows : (d + 1) * rows].astype(BF16) for d in range(n_tiles)]

    def spread_out(parts):
        return [shifted(part, "tiles", n_tiles, d) if d else part for d, part in enumerate(parts)]

    def stacked_shape(lanes, dtype=BF16):
        return jax.ShapeDtypeStruct((stack_rows, lanes.stop - lanes.start), dtype)

    def split_shapes(columns):
        return [
            jax.ShapeDtypeStruct((n_tiles * rows, columns), BF16),
            jax.ShapeDtypeStruct((stack_rows - n_tiles * rows, columns), BF16),
        ]

    numbers = jnp.stack([tile_rank, tile_row, tile_col])
    other_tables = others(numbers)
    other_ins = others(basis_in)
    other_outs = [others(basis_out[:, lanes]) for lanes in cuts]
    every = slice(0, BLK)

    partial, stacked = on_chip(
        functools.partial(opening_kernel, sizes),
        (place, [numbers]),
        (gather(sources), [basis_in], [basis_out]),
        [stacked_shape(every, F32), stacked_shape(every)],
        [pltpu.VMEM((stack_rows, width), BF16)],
        0,
        temporary,
        "far_own",
    )
    (near,) = near_field(rows, [stacked], near_blocks, near_slots, False)
    stacked, near = lax.optimization_barrier((stacked, near))
    (masked,) = on_chip(
        functools.partial(masked_kernel, sizes),
        (place, other_tables),
        (stacked, other_ins),
        [jax.ShapeDtypeStruct((stack_rows, (n_rhs - 1) * width), BF16)],
        [],
        0,
        temporary,
        "far_first_stage",
    )
    fields, parts = [], ()
    for lanes, outs in zip(cuts, other_outs):
        if parts:
            fields.append(finish(spread_out(parts), near, jacobi_inverse, cuts[len(fields)]))
        keep, send = on_chip(
            functools.partial(joining_kernel, lanes),
            (),
            (masked, partial, outs),
            split_shapes(lanes.stop - lanes.start),
            [],
            JOIN if parts else 0,
            temporary,
            "far_second_stage",
        )
        parts = reduced(keep, send)
    fields.append(finish(spread_out(parts), near, jacobi_inverse, cuts[-1]))

    tables = (place, [numbers] + other_tables)
    ins = [basis_in] + other_ins
    outs = [[basis_out] + arrays for arrays in other_outs]
    keep_shape, send_shape = split_shapes(BLK)
    send, stacked, kept = on_chip(
        functools.partial(sent_kernel, sizes, cuts),
        tables,
        ([gather(field) for field in fields], ins, outs),
        [send_shape, stacked_shape(every)]
        + [jax.ShapeDtypeStruct((n_tiles * rows, n_rhs * width), BF16)],
        [pltpu.VMEM((n_tiles * rows, n_rhs * width), BF16)] * (n_sub - 1),
        0,
        temporary,
        "far_sent",
    )
    (keep,) = on_chip(
        functools.partial(kept_kernel, cuts),
        (),
        (kept, outs),
        [keep_shape],
        [],
        KEPT,
        temporary,
        "far_kept",
    )
    near, first_result = near_field(rows, [stacked], near_blocks, near_slots, True)
    second_result = finish(spread_out(reduced(keep, send)), near, jacobi_inverse, every)
    return (first_result, second_result)


def solution(mesh):
    sizes = mesh.shape
    return jax.shard_map(
        functools.partial(local, sizes["tiles"], sizes["rhs"], sizes["sub"]),
        mesh=mesh,
        in_specs=(
            P("rhs", ("groups", "tiles", "sub")),
            P(("groups", "tiles", "rhs", "sub"), None, None),
            P(("groups", "tiles", "rhs", "sub"), None, None),
            P(("groups", "tiles", "rhs", "sub")),
            P(("groups", "tiles", "rhs", "sub")),
            P(("groups", "tiles", "rhs", "sub")),
            P(("groups", "tiles", "sub"), None, None, None),
            P(("groups", "tiles", "sub"), None),
            P(("groups", "tiles", "sub"), None, None),
        ),
        out_specs=(P("rhs", ("groups", "tiles", "sub")), P("rhs", ("groups", "tiles", "sub"))),
        check_vma=False,
    )
```

```python
import functools

import jax
import jax.numpy as jnp
from jax import lax
from jax.experimental import pallas as pl
from jax.experimental.pallas import tpu as pltpu
from jax.sharding import PartitionSpec as P

BLK = 512
RMAX = 64
JOIN = 10
KEPT = 10
JB = 128
NCHUNK = 256
BF16 = jnp.bfloat16
F32 = jnp.float32


def hint(us):
    return pl.CostEstimate(flops=int(us * 1e9) + 1, transcendentals=0, bytes_accessed=1)


CONTRACT_LAST = (((1,), (1,)), ((), ()))


def shifted(value, axis, size, amount):
    return lax.ppermute(value, axis, [(i, (i + amount) % size) for i in range(size)])


def on_chip(kernel, scalars, arrays, out_shapes, scratch, cost, limit, name):
    scalars, scalar_tree = jax.tree.flatten(scalars)
    arrays, array_tree = jax.tree.flatten(arrays)
    n_scalars, n_in, n_out = len(scalars), len(arrays), len(out_shapes)
    whole = pl.BlockSpec(memory_space=pltpu.VMEM)
    in_smem = pl.BlockSpec(memory_space=pltpu.SMEM)

    def body(*refs):
        numbers = jax.tree.unflatten(scalar_tree, refs[:n_scalars])
        inputs = jax.tree.unflatten(array_tree, refs[n_scalars : n_scalars + n_in])
        rest = refs[n_scalars + n_in :]
        kernel(numbers, inputs, rest[:n_out], rest[n_out:])

    moved = sum(a.size * a.dtype.itemsize for a in [*arrays, *out_shapes])
    return pl.pallas_call(
        body,
        out_shape=tuple(out_shapes),
        in_specs=[in_smem] * n_scalars + [whole] * n_in,
        out_specs=(whole,) * n_out,
        scratch_shapes=scratch,
        compiler_params=pltpu.CompilerParams(vmem_limit_bytes=limit + moved),
        cost_estimate=hint(cost),
        name=name,
    )(*scalars, *arrays)


def stack(pieces, stacked):
    rows = pieces[0].shape[0]
    for i, piece in enumerate(pieces):
        stacked[i * rows : (i + 1) * rows, :] = piece[...]


def spread(values):
    tile = lax.broadcasted_iota(jnp.int32, (1, NCHUNK), 1) // RMAX
    out = jnp.full((1, NCHUNK), values[0], jnp.int32)
    for i, value in enumerate(values[1:], 1):
        out = jnp.where(tile == i, value, out)
    return out


def slots_of(place, table, tiles, sizes):
    n_tiles, n_sub = sizes
    z, s = place[0], place[1]
    lane = lax.broadcasted_iota(jnp.int32, (1, NCHUNK), 1) % RMAX
    column = spread(
        [
            lax.rem(s + n_sub - lax.rem(table[2, t], n_sub), n_sub) * n_tiles
            + lax.rem(z + n_tiles - lax.div(table[2, t], n_sub), n_tiles)
            for t in tiles
        ]
    )
    target = spread(
        [
            lax.rem(lax.rem(table[1, t], n_sub) + n_sub - s, n_sub) * n_tiles
            + lax.rem(lax.div(table[1, t], n_sub) + n_tiles - z, n_tiles)
            for t in tiles
        ]
    )
    return column, jnp.where(lane < spread([table[0, t] for t in tiles]), target, -1)


def first_stage(numbers, sizes, stacked, ins, lanes, previous, coeff, masked):
    place, tables = numbers
    n_tiles, n_sub = sizes
    rows = stacked.shape[0] // (n_tiles * n_sub)
    first = 0
    for table, basis in zip(tables, ins):
        for start in range(0, basis.shape[0], NCHUNK):
            tiles = range(start // RMAX, (start + NCHUNK) // RMAX)
            target = slots_of(place, table, tiles, sizes)[1]
            found = []
            for t in tiles:
                block = table[2, t]
                slot = lax.rem(place[1] + n_sub - lax.rem(block, n_sub), n_sub) * n_tiles
                slot += lax.rem(place[0] + n_tiles - lax.div(block, n_sub), n_tiles)
                begin = pl.multiple_of(slot * rows, rows)
                found.append(
                    lax.dot_general(
                        stacked[pl.ds(begin, rows), :],
                        basis[t * RMAX : (t + 1) * RMAX, :],
                        CONTRACT_LAST,
                        preferred_element_type=F32,
                    )
                )
            chosen = jnp.concatenate(found, axis=1)
            there = slice(first, first + NCHUNK)
            for i, part in enumerate(masked):
                held = part.shape[0] // rows
                for piece in range(held):
                    part[piece * rows : (piece + 1) * rows, there] = jnp.where(
                        target == i * held + piece, chosen, 0.0
                    ).astype(BF16)
            first += NCHUNK


def second_stage(masked, outs, lanes, total):
    first = 0
    for basis in outs:
        values = basis[...] if basis.shape[1] == lanes.stop - lanes.start else basis[:, lanes]
        added = jnp.dot(
            masked[:, first : first + basis.shape[0]], values, preferred_element_type=F32
        )
        total = added if total is None else total + added
        first += basis.shape[0]
    return total


def split_sums(total, keep_ref, send_ref, lanes):
    kept = keep_ref.shape[0]
    total = total.astype(BF16)
    keep_ref[:, lanes] = total[:kept]
    send_ref[:, lanes] = total[kept:]


def opening_kernel(sizes, numbers, inputs, results, scratch):
    pieces, ins, outs = inputs
    total, stacked = results
    (masked,) = scratch
    every = slice(0, BLK)
    stack(pieces, stacked)
    first_stage(numbers, sizes, stacked, ins, every, None, None, [masked])
    total[...] = second_stage(masked, outs, every, None)


def masked_kernel(sizes, numbers, inputs, results, scratch):
    stacked, ins = inputs
    first_stage(numbers, sizes, stacked, ins, slice(0, BLK), None, None, results)


def joining_kernel(lanes, numbers, inputs, results, scratch):
    masked, partial, outs = inputs
    total = second_stage(masked, outs, lanes, partial[:, lanes])
    split_sums(total, *results, slice(0, lanes.stop - lanes.start))


def sent_kernel(sizes, lanes, numbers, inputs, results, scratch):
    pieces_by_lanes, ins, outs_by_lanes = inputs
    send_ref, stacked, *masked = results
    for here, pieces in zip(lanes, pieces_by_lanes):
        stack(pieces, stacked.at[:, here])
    first_stage(numbers, sizes, stacked, ins, slice(0, BLK), None, None, [*masked, *scratch])
    size = masked[0].shape[0]
    for here, outs in zip(lanes, outs_by_lanes):
        for i, part in enumerate(scratch):
            total = second_stage(part, outs, here, None)
            send_ref[i * size : (i + 1) * size, here] = total.astype(BF16)


def kept_kernel(lanes, numbers, inputs, results, scratch):
    masked, outs_by_lanes = inputs
    for here, outs in zip(lanes, outs_by_lanes):
        results[0][:, here] = second_stage(masked, outs, here, None).astype(BF16)


def near_kernel(n_stacks, per_step, slot_ref, *refs):
    stacks, (blocks_ref, out_ref, *own, total) = refs[:n_stacks], refs[n_stacks:]
    rows = out_ref.shape[0]
    step = pl.program_id(0)

    @pl.when(step == 0)
    def _():
        total[...] = jnp.zeros_like(total)

    added = total[...]
    for k in range(per_step):
        start = pl.multiple_of(slot_ref[step * per_step + k] * rows, rows)
        first = 0
        for stacked in stacks:
            width = stacked.shape[1]
            added += lax.dot_general(
                stacked[pl.ds(start, rows), :],
                blocks_ref[k, :, first : first + width],
                CONTRACT_LAST,
                preferred_element_type=F32,
            )
            first += width
    total[...] = added

    @pl.when(step == pl.num_programs(0) - 1)
    def _():
        out_ref[...] = total[...]
        for ref in own:
            first = 0
            for stacked in stacks:
                ref[:, first : first + stacked.shape[1]] = stacked[:rows, :]
                first += stacked.shape[1]


def near_field(rows, stacks, near_blocks, slots, with_own):
    near = near_blocks.shape[0]
    per_step = 4 if near % 4 == 0 else 1
    whole = pl.BlockSpec(memory_space=pltpu.VMEM)
    out_shape = [jax.ShapeDtypeStruct((rows, BLK), F32)]
    if with_own:
        out_shape.append(jax.ShapeDtypeStruct((rows, BLK), BF16))
    return pl.pallas_call(
        functools.partial(near_kernel, len(stacks), per_step),
        out_shape=tuple(out_shape),
        grid_spec=pltpu.PrefetchScalarGridSpec(
            num_scalar_prefetch=1,
            grid=(near // per_step,),
            in_specs=[whole] * len(stacks)
            + [pl.BlockSpec((per_step, BLK, BLK), lambda step, slot: (step, 0, 0))],
            out_specs=(whole,) * len(out_shape),
            scratch_shapes=[pltpu.VMEM((rows, BLK), F32)],
        ),
        compiler_params=pltpu.CompilerParams(vmem_limit_bytes=14 << 20),
        cost_estimate=hint(0),
        name="near_field",
    )(slots, *stacks, near_blocks)


def combine_kernel(numbers, inputs, results, scratch):
    keep, received = inputs
    rows = results[0].shape[0]
    for d, result in enumerate(results):
        here = slice(d * rows, (d + 1) * rows)
        total = keep[here, :].astype(F32)
        for part in received:
            total += part[here, :].astype(F32)
        result[...] = total.astype(BF16)


def finish_kernel(lanes, numbers, inputs, results, scratch):
    sums, near_ref, jacobi_ref = inputs
    total = near_ref[:, lanes]
    for part in sums:
        total += part[...].astype(F32)
    field = total.astype(BF16)
    for start in range(0, lanes.stop - lanes.start, JB):
        here = slice(start, start + JB)
        results[0][:, here] = lax.dot_general(
            field[:, here],
            jacobi_ref[(lanes.start + start) // JB],
            CONTRACT_LAST,
            preferred_element_type=F32,
        ).astype(BF16)


def finish(sums, near, jacobi_inverse, lanes):
    return on_chip(
        functools.partial(finish_kernel, lanes),
        (),
        (sums, near, jacobi_inverse),
        [jax.ShapeDtypeStruct(sums[0].shape, BF16)],
        [],
        0,
        2 << 20,
        "finish",
    )[0]


def local(
    n_tiles,
    n_rhs,
    n_sub,
    sources,
    basis_out,
    basis_in,
    tile_rank,
    tile_row,
    tile_col,
    near_blocks,
    near_col,
    jacobi_inverse,
):
    z = lax.axis_index("tiles")
    s = lax.axis_index("sub")
    rows = sources.shape[0]
    basis_in = basis_in.reshape(-1, BLK)
    basis_out = basis_out.reshape(-1, BLK)
    width = basis_in.shape[0]
    sizes = (n_tiles, n_sub)
    n_pieces = n_tiles * n_sub
    stack_rows = n_pieces * rows
    cuts = [slice(0, BLK // 2), slice(BLK // 2, BLK)]
    place = jnp.stack([z, s])
    near_slots = (s - near_col[0] % n_sub) % n_sub * n_tiles + (z - near_col[0] // n_sub) % n_tiles
    near_blocks = near_blocks[0]
    temporary = stack_rows * (16 * BLK + 8 * NCHUNK) + (2 << 20)

    def gather(field):
        along = [field] + [shifted(field, "tiles", n_tiles, d) for d in range(1, n_tiles)]
        pieces = list(along)
        for e in range(1, n_sub):
            pieces += [shifted(piece, "sub", n_sub, e) for piece in along]
        return pieces

    def others(array):
        return [shifted(array, "rhs", n_rhs, e) for e in range(1, n_rhs)]

    def reduced(keep, send):
        size = n_tiles * rows
        received = [
            shifted(send[(e - 1) * size : e * size], "sub", n_sub, e) for e in range(1, n_sub)
        ]
        return on_chip(
            combine_kernel,
            (),
            (keep, received),
            [jax.ShapeDtypeStruct((rows, keep.shape[1]), BF16)] * n_tiles,
            [],
            0,
            2 << 20,
            "combine",
        )

    def spread_out(parts):
        return [shifted(part, "tiles", n_tiles, d) if d else part for d, part in enumerate(parts)]

    def stacked_shape(lanes, dtype=BF16):
        return jax.ShapeDtypeStruct((stack_rows, lanes.stop - lanes.start), dtype)

    def split_shapes(columns):
        return [
            jax.ShapeDtypeStruct((n_tiles * rows, columns), BF16),
            jax.ShapeDtypeStruct((stack_rows - n_tiles * rows, columns), BF16),
        ]

    numbers = jnp.stack([tile_rank, tile_row, tile_col])
    other_tables = others(numbers)
    other_ins = others(basis_in)
    other_outs = [others(basis_out[:, lanes]) for lanes in cuts]
    every = slice(0, BLK)

    partial, stacked = on_chip(
        functools.partial(opening_kernel, sizes),
        (place, [numbers]),
        (gather(sources), [basis_in], [basis_out]),
        [stacked_shape(every, F32), stacked_shape(every)],
        [pltpu.VMEM((stack_rows, width), BF16)],
        0,
        temporary,
        "far_own",
    )
    (near,) = near_field(rows, [stacked], near_blocks, near_slots, False)
    stacked, near = lax.optimization_barrier((stacked, near))
    (masked,) = on_chip(
        functools.partial(masked_kernel, sizes),
        (place, other_tables),
        (stacked, other_ins),
        [jax.ShapeDtypeStruct((stack_rows, (n_rhs - 1) * width), BF16)],
        [],
        0,
        temporary,
        "far_first_stage",
    )
    fields, parts = [], ()
    for lanes, outs in zip(cuts, other_outs):
        if parts:
            fields.append(finish(spread_out(parts), near, jacobi_inverse, cuts[len(fields)]))
        keep, send = on_chip(
            functools.partial(joining_kernel, lanes),
            (),
            (masked, partial, outs),
            split_shapes(lanes.stop - lanes.start),
            [],
            JOIN if parts else 0,
            temporary,
            "far_second_stage",
        )
        parts = reduced(keep, send)
    fields.append(finish(spread_out(parts), near, jacobi_inverse, cuts[-1]))

    tables = (place, [numbers] + other_tables)
    ins = [basis_in] + other_ins
    outs = [[basis_out] + arrays for arrays in other_outs]
    keep_shape, send_shape = split_shapes(BLK)
    send, stacked, kept = on_chip(
        functools.partial(sent_kernel, sizes, cuts),
        tables,
        ([gather(field) for field in fields], ins, outs),
        [send_shape, stacked_shape(every)]
        + [jax.ShapeDtypeStruct((n_tiles * rows, n_rhs * width), BF16)],
        [pltpu.VMEM((n_tiles * rows, n_rhs * width), BF16)] * (n_sub - 1),
        0,
        temporary,
        "far_sent",
    )
    (keep,) = on_chip(
        functools.partial(kept_kernel, cuts),
        (),
        (kept, outs),
        [keep_shape],
        [],
        KEPT,
        temporary,
        "far_kept",
    )
    near, first_result = near_field(rows, [stacked], near_blocks, near_slots, True)
    second_result = finish(spread_out(reduced(keep, send)), near, jacobi_inverse, every)
    return (first_result, second_result)


def solution(mesh):
    sizes = mesh.shape
    return jax.shard_map(
        functools.partial(local, sizes["tiles"], sizes["rhs"], sizes["sub"]),
        mesh=mesh,
        in_specs=(
            P("rhs", ("groups", "tiles", "sub")),
            P(("groups", "tiles", "rhs", "sub"), None, None),
            P(("groups", "tiles", "rhs", "sub"), None, None),
            P(("groups", "tiles", "rhs", "sub")),
            P(("groups", "tiles", "rhs", "sub")),
            P(("groups", "tiles", "rhs", "sub")),
            P(("groups", "tiles", "sub"), None, None, None),
            P(("groups", "tiles", "sub"), None),
            P(("groups", "tiles", "sub"), None, None),
        ),
        out_specs=(P("rhs", ("groups", "tiles", "sub")), P("rhs", ("groups", "tiles", "sub"))),
        check_vma=False,
    )
```

```python
import functools

import jax
import jax.numpy as jnp
from jax import lax
from jax.experimental import pallas as pl
from jax.experimental.pallas import tpu as pltpu
from jax.sharding import PartitionSpec as P

BLK = 512
RMAX = 64
JOIN = 10
KEPT = 10
JB = 128
NCHUNK = 256
BF16 = jnp.bfloat16
F32 = jnp.float32


def hint(us):
    return pl.CostEstimate(flops=int(us * 1e9) + 1, transcendentals=0, bytes_accessed=1)


CONTRACT_LAST = (((1,), (1,)), ((), ()))


def shifted(value, axis, size, amount):
    return lax.ppermute(value, axis, [(i, (i + amount) % size) for i in range(size)])


def on_chip(kernel, scalars, arrays, out_shapes, scratch, cost, limit, name):
    scalars, scalar_tree = jax.tree.flatten(scalars)
    arrays, array_tree = jax.tree.flatten(arrays)
    n_scalars, n_in, n_out = len(scalars), len(arrays), len(out_shapes)
    whole = pl.BlockSpec(memory_space=pltpu.VMEM)
    in_smem = pl.BlockSpec(memory_space=pltpu.SMEM)

    def body(*refs):
        numbers = jax.tree.unflatten(scalar_tree, refs[:n_scalars])
        inputs = jax.tree.unflatten(array_tree, refs[n_scalars : n_scalars + n_in])
        rest = refs[n_scalars + n_in :]
        kernel(numbers, inputs, rest[:n_out], rest[n_out:])

    moved = sum(a.size * a.dtype.itemsize for a in [*arrays, *out_shapes])
    return pl.pallas_call(
        body,
        out_shape=tuple(out_shapes),
        in_specs=[in_smem] * n_scalars + [whole] * n_in,
        out_specs=(whole,) * n_out,
        scratch_shapes=scratch,
        compiler_params=pltpu.CompilerParams(vmem_limit_bytes=limit + moved),
        cost_estimate=hint(cost),
        name=name,
    )(*scalars, *arrays)


def stack(pieces, stacked):
    rows = pieces[0].shape[0]
    for i, piece in enumerate(pieces):
        stacked[i * rows : (i + 1) * rows, :] = piece[...]


def spread(values):
    tile = lax.broadcasted_iota(jnp.int32, (1, NCHUNK), 1) // RMAX
    out = jnp.full((1, NCHUNK), values[0], jnp.int32)
    for i, value in enumerate(values[1:], 1):
        out = jnp.where(tile == i, value, out)
    return out


def slots_of(place, table, tiles, sizes):
    n_tiles, n_sub = sizes
    z, s = place[0], place[1]
    lane = lax.broadcasted_iota(jnp.int32, (1, NCHUNK), 1) % RMAX
    column = spread(
        [
            lax.rem(s + n_sub - lax.rem(table[2, t], n_sub), n_sub) * n_tiles
            + lax.rem(z + n_tiles - lax.div(table[2, t], n_sub), n_tiles)
            for t in tiles
        ]
    )
    target = spread(
        [
            lax.rem(lax.rem(table[1, t], n_sub) + n_sub - s, n_sub) * n_tiles
            + lax.rem(lax.div(table[1, t], n_sub) + n_tiles - z, n_tiles)
            for t in tiles
        ]
    )
    return column, jnp.where(lane < spread([table[0, t] for t in tiles]), target, -1)


def first_stage(numbers, sizes, stacked, ins, lanes, previous, coeff, masked):
    place, tables = numbers
    n_tiles, n_sub = sizes
    rows = stacked.shape[0] // (n_tiles * n_sub)
    first = 0
    for table, basis in zip(tables, ins):
        for start in range(0, basis.shape[0], NCHUNK):
            tiles = range(start // RMAX, (start + NCHUNK) // RMAX)
            target = slots_of(place, table, tiles, sizes)[1]
            found = []
            for t in tiles:
                block = table[2, t]
                slot = lax.rem(place[1] + n_sub - lax.rem(block, n_sub), n_sub) * n_tiles
                slot += lax.rem(place[0] + n_tiles - lax.div(block, n_sub), n_tiles)
                begin = pl.multiple_of(slot * rows, rows)
                found.append(
                    lax.dot_general(
                        stacked[pl.ds(begin, rows), :],
                        basis[t * RMAX : (t + 1) * RMAX, :],
                        CONTRACT_LAST,
                        preferred_element_type=F32,
                    )
                )
            chosen = jnp.concatenate(found, axis=1)
            there = slice(first, first + NCHUNK)
            for i, part in enumerate(masked):
                held = part.shape[0] // rows
                for piece in range(held):
                    part[piece * rows : (piece + 1) * rows, there] = jnp.where(
                        target == i * held + piece, chosen, 0.0
                    ).astype(BF16)
            first += NCHUNK


def second_stage(masked, outs, lanes, total):
    first = 0
    for basis in outs:
        values = basis[...] if basis.shape[1] == lanes.stop - lanes.start else basis[:, lanes]
        added = jnp.dot(
            masked[:, first : first + basis.shape[0]], values, preferred_element_type=F32
        )
        total = added if total is None else total + added
        first += basis.shape[0]
    return total


def split_sums(total, keep_ref, send_ref, lanes):
    kept = keep_ref.shape[0]
    total = total.astype(BF16)
    keep_ref[:, lanes] = total[:kept]
    send_ref[:, lanes] = total[kept:]


def opening_kernel(sizes, numbers, inputs, results, scratch):
    pieces, ins, outs = inputs
    total, stacked = results
    (masked,) = scratch
    every = slice(0, BLK)
    stack(pieces, stacked)
    first_stage(numbers, sizes, stacked, ins, every, None, None, [masked])
    total[...] = second_stage(masked, outs, every, None)


def masked_kernel(sizes, numbers, inputs, results, scratch):
    stacked, ins = inputs
    first_stage(numbers, sizes, stacked, ins, slice(0, BLK), None, None, results)


def joining_kernel(lanes, numbers, inputs, results, scratch):
    masked, partial, outs = inputs
    total = second_stage(masked, outs, lanes, partial[:, lanes])
    split_sums(total, *results, slice(0, lanes.stop - lanes.start))


def sent_kernel(sizes, lanes, numbers, inputs, results, scratch):
    pieces_by_lanes, ins, outs_by_lanes = inputs
    low_ref, high_ref, stacked, *masked = results
    for here, pieces in zip(lanes, pieces_by_lanes):
        stack(pieces, stacked.at[:, here])
    first_stage(numbers, sizes, stacked, ins, slice(0, BLK), None, None, [*masked, *scratch])
    size = masked[0].shape[0]
    for here, outs in zip(lanes, outs_by_lanes):
        for i, part in enumerate(scratch):
            total = second_stage(part, outs, here, None)
            total, half = total.astype(BF16), size // 2
            low_ref[i * half : (i + 1) * half, here] = total[:half]
            high_ref[i * half : (i + 1) * half, here] = total[half:]


def kept_kernel(lanes, numbers, inputs, results, scratch):
    masked, outs_by_lanes = inputs
    for here, outs in zip(lanes, outs_by_lanes):
        results[0][:, here] = second_stage(masked, outs, here, None).astype(BF16)


def near_kernel(n_stacks, per_step, slot_ref, *refs):
    stacks, (blocks_ref, out_ref, *own, total) = refs[:n_stacks], refs[n_stacks:]
    rows = out_ref.shape[0]
    step = pl.program_id(0)

    @pl.when(step == 0)
    def _():
        total[...] = jnp.zeros_like(total)

    added = total[...]
    for k in range(per_step):
        start = pl.multiple_of(slot_ref[step * per_step + k] * rows, rows)
        first = 0
        for stacked in stacks:
            width = stacked.shape[1]
            added += lax.dot_general(
                stacked[pl.ds(start, rows), :],
                blocks_ref[k, :, first : first + width],
                CONTRACT_LAST,
                preferred_element_type=F32,
            )
            first += width
    total[...] = added

    @pl.when(step == pl.num_programs(0) - 1)
    def _():
        out_ref[...] = total[...]
        for ref in own:
            first = 0
            for stacked in stacks:
                ref[:, first : first + stacked.shape[1]] = stacked[:rows, :]
                first += stacked.shape[1]


def near_field(rows, stacks, near_blocks, slots, with_own):
    near = near_blocks.shape[0]
    per_step = 4 if near % 4 == 0 else 1
    whole = pl.BlockSpec(memory_space=pltpu.VMEM)
    out_shape = [jax.ShapeDtypeStruct((rows, BLK), F32)]
    if with_own:
        out_shape.append(jax.ShapeDtypeStruct((rows, BLK), BF16))
    return pl.pallas_call(
        functools.partial(near_kernel, len(stacks), per_step),
        out_shape=tuple(out_shape),
        grid_spec=pltpu.PrefetchScalarGridSpec(
            num_scalar_prefetch=1,
            grid=(near // per_step,),
            in_specs=[whole] * len(stacks)
            + [pl.BlockSpec((per_step, BLK, BLK), lambda step, slot: (step, 0, 0))],
            out_specs=(whole,) * len(out_shape),
            scratch_shapes=[pltpu.VMEM((rows, BLK), F32)],
        ),
        compiler_params=pltpu.CompilerParams(vmem_limit_bytes=14 << 20),
        cost_estimate=hint(0),
        name="near_field",
    )(slots, *stacks, near_blocks)


def finish_kernel(lanes, numbers, inputs, results, scratch):
    sums, near_ref, jacobi_ref = inputs
    total = near_ref[:, lanes]
    for part in sums:
        total += part[...].astype(F32)
    field = total.astype(BF16)
    for start in range(0, lanes.stop - lanes.start, JB):
        here = slice(start, start + JB)
        results[0][:, here] = lax.dot_general(
            field[:, here],
            jacobi_ref[(lanes.start + start) // JB],
            CONTRACT_LAST,
            preferred_element_type=F32,
        ).astype(BF16)


def finish(sums, near, jacobi_inverse, lanes):
    return on_chip(
        functools.partial(finish_kernel, lanes),
        (),
        (sums, near, jacobi_inverse),
        [jax.ShapeDtypeStruct(sums[0].shape, BF16)],
        [],
        0,
        2 << 20,
        "finish",
    )[0]


def local(
    n_tiles,
    n_rhs,
    n_sub,
    sources,
    basis_out,
    basis_in,
    tile_rank,
    tile_row,
    tile_col,
    near_blocks,
    near_col,
    jacobi_inverse,
):
    z = lax.axis_index("tiles")
    s = lax.axis_index("sub")
    rows = sources.shape[0]
    basis_in = basis_in.reshape(-1, BLK)
    basis_out = basis_out.reshape(-1, BLK)
    width = basis_in.shape[0]
    sizes = (n_tiles, n_sub)
    n_pieces = n_tiles * n_sub
    stack_rows = n_pieces * rows
    cuts = [slice(0, BLK // 2), slice(BLK // 2, BLK)]
    place = jnp.stack([z, s])
    near_slots = (s - near_col[0] % n_sub) % n_sub * n_tiles + (z - near_col[0] // n_sub) % n_tiles
    near_blocks = near_blocks[0]
    temporary = stack_rows * (16 * BLK + 8 * NCHUNK) + (2 << 20)

    def gather(field):
        along = [field] + [shifted(field, "tiles", n_tiles, d) for d in range(1, n_tiles)]
        pieces = list(along)
        for e in range(1, n_sub):
            pieces += [shifted(piece, "sub", n_sub, e) for piece in along]
        return pieces

    def others(array):
        return [shifted(array, "rhs", n_rhs, e) for e in range(1, n_rhs)]

    def reduced(keep, send):
        total = keep.astype(F32)
        for e in range(1, n_sub):
            size = n_tiles * rows
            total += shifted(send[(e - 1) * size : e * size], "sub", n_sub, e).astype(F32)
        return [total[d * rows : (d + 1) * rows].astype(BF16) for d in range(n_tiles)]

    def spread_out(parts):
        return [shifted(part, "tiles", n_tiles, d) if d else part for d, part in enumerate(parts)]

    def stacked_shape(lanes, dtype=BF16):
        return jax.ShapeDtypeStruct((stack_rows, lanes.stop - lanes.start), dtype)

    def split_shapes(columns):
        return [
            jax.ShapeDtypeStruct((n_tiles * rows, columns), BF16),
            jax.ShapeDtypeStruct((stack_rows - n_tiles * rows, columns), BF16),
        ]

    numbers = jnp.stack([tile_rank, tile_row, tile_col])
    other_tables = others(numbers)
    other_ins = others(basis_in)
    other_outs = [others(basis_out[:, lanes]) for lanes in cuts]
    every = slice(0, BLK)

    partial, stacked = on_chip(
        functools.partial(opening_kernel, sizes),
        (place, [numbers]),
        (gather(sources), [basis_in], [basis_out]),
        [stacked_shape(every, F32), stacked_shape(every)],
        [pltpu.VMEM((stack_rows, width), BF16)],
        0,
        temporary,
        "far_own",
    )
    (near,) = near_field(rows, [stacked], near_blocks, near_slots, False)
    stacked, near = lax.optimization_barrier((stacked, near))
    (masked,) = on_chip(
        functools.partial(masked_kernel, sizes),
        (place, other_tables),
        (stacked, other_ins),
        [jax.ShapeDtypeStruct((stack_rows, (n_rhs - 1) * width), BF16)],
        [],
        0,
        temporary,
        "far_first_stage",
    )
    fields, parts = [], ()
    for lanes, outs in zip(cuts, other_outs):
        if parts:
            fields.append(finish(spread_out(parts), near, jacobi_inverse, cuts[len(fields)]))
        keep, send = on_chip(
            functools.partial(joining_kernel, lanes),
            (),
            (masked, partial, outs),
            split_shapes(lanes.stop - lanes.start),
            [],
            JOIN if parts else 0,
            temporary,
            "far_second_stage",
        )
        parts = reduced(keep, send)
    fields.append(finish(spread_out(parts), near, jacobi_inverse, cuts[-1]))

    tables = (place, [numbers] + other_tables)
    ins = [basis_in] + other_ins
    outs = [[basis_out] + arrays for arrays in other_outs]
    keep_shape, send_shape = split_shapes(BLK)
    half_shape = jax.ShapeDtypeStruct((send_shape.shape[0] // 2, BLK), BF16)
    low, high, stacked, kept = on_chip(
        functools.partial(sent_kernel, sizes, cuts),
        tables,
        ([gather(field) for field in fields], ins, outs),
        [half_shape, half_shape, stacked_shape(every)]
        + [jax.ShapeDtypeStruct((n_tiles * rows, n_rhs * width), BF16)],
        [pltpu.VMEM((n_tiles * rows, n_rhs * width), BF16)] * (n_sub - 1),
        0,
        temporary,
        "far_sent",
    )
    (keep,) = on_chip(
        functools.partial(kept_kernel, cuts),
        (),
        (kept, outs),
        [keep_shape],
        [],
        KEPT,
        temporary,
        "far_kept",
    )
    near, first_result = near_field(rows, [stacked], near_blocks, near_slots, True)
    half = n_tiles * rows // 2
    parts = []
    for held, send in ((keep[:half], low), (keep[half:], high)):
        total = held.astype(F32)
        for e in range(1, n_sub):
            here = slice((e - 1) * half, e * half)
            total += shifted(send[here], "sub", n_sub, e).astype(F32)
        parts += [total[d * rows : (d + 1) * rows].astype(BF16) for d in range(n_tiles // 2)]
    second_result = finish(spread_out(parts), near, jacobi_inverse, every)
    return (first_result, second_result)


def solution(mesh):
    sizes = mesh.shape
    return jax.shard_map(
        functools.partial(local, sizes["tiles"], sizes["rhs"], sizes["sub"]),
        mesh=mesh,
        in_specs=(
            P("rhs", ("groups", "tiles", "sub")),
            P(("groups", "tiles", "rhs", "sub"), None, None),
            P(("groups", "tiles", "rhs", "sub"), None, None),
            P(("groups", "tiles", "rhs", "sub")),
            P(("groups", "tiles", "rhs", "sub")),
            P(("groups", "tiles", "rhs", "sub")),
            P(("groups", "tiles", "sub"), None, None, None),
            P(("groups", "tiles", "sub"), None),
            P(("groups", "tiles", "sub"), None, None),
        ),
        out_specs=(P("rhs", ("groups", "tiles", "sub")), P("rhs", ("groups", "tiles", "sub"))),
        check_vma=False,
    )
```
